256 devices in a mesh: frame: 256 (over x, z, y, core).
Axes of the slice: x: 4, y: 4, z: 8, core: 2. Of those that a mesh axis runs over, the one named last changes fastest.
Arguments:
- diag_even: float32 [512, 256, 256], P('frame'), may hold values from -0.375 to 0.375
- inv_odd: float32 [512, 256, 256], P('frame'), as said below
- coupling: float32 [1024, 256, 256], P('frame'), may hold values from -0.375 to 0.375
- arrow_blocks: float32 [1024, 512, 256], P('frame'), as said below
- arrow_tip: float32 [512, 512], P('frame'), may hold values from -6 to 6
Outputs:
- diag_new: float32 [512, 256, 256], P('frame')
- couple_new: float32 [512, 256, 256], P('frame')
- arrow_new: float32 [512, 512, 256], P('frame')
- tip_new: float32 [512, 512], P('frame')
The draws below stay inside these ranges and needn't reach their ends.
Inputs may be any that keep to these rules, and one draw needn't show every extreme that they name: `inv_odd`: each block is symmetric, with a diagonal near 1 and small off-diagonal entries. `arrow_blocks`: Real-valued entries of order 256 ** -0.5 or smaller.
All inputs are finite; a program needn't handle non-finite values.
Results may differ from the reference program's by a relative error of at most 0.000076.
Values sent between devices are 32-bit elements; how exact they have to be, the bound alone decides.
No kernel may reach another device: no remote copies, remote signals or barrier semaphores. Data moves between devices by JAX's collectives and lax.ppermute only.
A program may use at most 64 MiB of HBM per device.

```python
import jax
import jax.numpy as jnp
from jax import lax

B = 256
A = 512
FR_DEV = 4
FRAMES = 1024


def draw_inv_odd(key, part):
    shape = (FRAMES // 2, B, B)
    noise = jax.random.normal(key, shape, jnp.float32)
    sym = 0.5 * (noise + jnp.swapaxes(noise, 1, 2)) / jnp.sqrt(2.0 * B)
    return jnp.eye(B, dtype=jnp.float32)[None] + sym


def draw_arrow_blocks(key, part):
    devices_count = FRAMES // FR_DEV
    key_pattern = jax.random.fold_in(key, 11)
    key_gain = jax.random.fold_in(key, 12)
    key_noise = jax.random.fold_in(key, 13)
    key_pair = jax.random.fold_in(key, 14)
    sigma = 1.0 / jnp.sqrt(jnp.float32(B) * jnp.float32(devices_count))
    pattern = jax.random.truncated_normal(key_pattern, -6.0, 6.0, (A, B), jnp.float32) / jnp.sqrt(jnp.float32(B))
    factor = jnp.exp(jax.random.uniform(key_gain, (FRAMES,), jnp.float32, minval=jnp.log(0.7), maxval=jnp.log(1.4)))
    noise = jax.random.truncated_normal(key_noise, -6.0, 6.0, (FRAMES, A, B), jnp.float32) * sigma
    position = jnp.arange(FRAMES, dtype=jnp.float32)
    rising = jnp.sqrt(1.0 + 2.0 * position / jnp.float32(FRAMES)) * factor
    gains = rising / jnp.sqrt(jnp.float32(FRAMES // 2))
    pairing = jax.random.permutation(key_pair, devices_count).astype(jnp.int32)
    owner = (jnp.arange(FRAMES, dtype=jnp.int32) // FR_DEV).astype(jnp.int32)
    target = pairing[owner]
    row_block = (jnp.arange(A, dtype=jnp.int32) // (A // devices_count)).astype(jnp.int32)
    boost = jnp.where(row_block[None, :] == target[:, None], 3.0, 1.0).astype(jnp.float32)
    blocks = gains[:, None, None] * pattern[None] + noise
    return blocks * boost[:, :, None]


def levels(rng, dims, split, least, high):
    gain, own = 1.0, jax.random.fold_in(rng, 6)
    for axis_at, blocks in split:
        heights = jnp.exp(jax.random.uniform(jax.random.fold_in(own, axis_at), (blocks,), jnp.float32, least / len(split), high / len(split)))
        gain = gain * jnp.repeat(heights, dims[axis_at] // blocks).reshape([-1 if axis == axis_at else 1 for axis in range(len(dims))])
    return gain


def scatter_about(rng, extent, scale, limit, cuts=(), held_as=jnp.bfloat16):
    array = jax.random.normal(rng, extent, jnp.float32) * scale
    if len(cuts) > 0:
        array = levels(rng, extent, cuts, -0.22, 0.18) * array
    return jnp.clip(array, min=-limit, max=limit).astype(held_as)


def setup_inputs(seed: int = 0) -> dict:
    keys = jax.random.split(jax.random.key(seed), 6)
    diag_even = scatter_about(keys[0], (FRAMES // 2, B, B), B ** -0.5, 0.375, ((0, 256),), jnp.float32)
    inv_odd = draw_inv_odd(jax.random.fold_in(keys[5], 71), 0)
    coupling = scatter_about(keys[2], (FRAMES, B, B), B ** -0.5, 0.375, ((0, 256),), jnp.float32)
    arrow_blocks = draw_arrow_blocks(jax.random.fold_in(keys[5], 71), 0)
    arrow_tip = scatter_about(keys[4], (A, A), 0.5, 6.0, ((0, 256),), jnp.float32)
    return {"diag_even": diag_even, "inv_odd": inv_odd, "coupling": coupling, "arrow_blocks": arrow_blocks, "arrow_tip": arrow_tip}


def reference(diag_even, inv_odd, coupling, arrow_blocks, arrow_tip):
    highest = lax.Precision.HIGHEST
    half_count = inv_odd.shape[0]
    order = coupling.shape[1]
    width = arrow_blocks.shape[1]
    linked = coupling.reshape(half_count, 2, order, order)
    link_prev = linked[:, 0]
    link_next = linked[:, 1]
    paired = arrow_blocks.reshape(half_count, 2, width, order)
    arrow_even = paired[:, 0]
    arrow_odd = paired[:, 1]
    left_prod = jnp.matmul(link_prev, inv_odd, precision=highest)
    inv_next = jnp.matmul(inv_odd, link_next, precision=highest)
    arrow_inv = jnp.matmul(arrow_odd, inv_odd, precision=highest)
    diag_left = jnp.matmul(left_prod, jnp.swapaxes(link_prev, 1, 2), precision=highest)
    diag_right = jnp.matmul(jnp.swapaxes(link_next, 1, 2), inv_next, precision=highest)
    couple_new = -jnp.matmul(left_prod, link_next, precision=highest)
    arrow_left = jnp.matmul(arrow_inv, jnp.swapaxes(link_prev, 1, 2), precision=highest)
    arrow_right = jnp.matmul(arrow_odd, inv_next, precision=highest)
    tip_terms = jnp.einsum("hab,hcb->ac", arrow_inv, arrow_odd, precision=highest)
    diag_shift = jnp.concatenate([jnp.zeros((1, order, order), jnp.float32), diag_right[:-1]], axis=0)
    arrow_shift = jnp.concatenate([jnp.zeros((1, width, order), jnp.float32), arrow_right[:-1]], axis=0)
    diag_new = diag_even - diag_left - diag_shift
    arrow_new = arrow_even - arrow_left - arrow_shift
    tip_new = arrow_tip - tip_terms
    return diag_new, couple_new, arrow_new, tip_new
```

```python
import jax
import jax.numpy as jnp
from jax import lax
from jax.sharding import Mesh
from jax.sharding import PartitionSpec as P

AXES = ("x", "z", "y", "c")
SIZES = (4, 8, 4, 2)


def shifted(x, by):
    count = 1
    for size in SIZES:
        count *= size
    pairs = [(i, i + by) for i in range(count) if 0 <= i + by < count]
    return lax.ppermute(x, AXES, pairs)


def product(left, right):
    return jnp.matmul(left, right, precision=lax.Precision.HIGHEST)


def scattered_sum(part):
    rows, cols = part.shape
    nx, nz, ny, nc = SIZES
    own = rows // (nx * nz * ny * nc)
    part = part.reshape(nx, nz, ny, nc, own, cols)
    part = part.transpose(3, 0, 2, 4, 1, 5)
    core = lax.axis_index("c")
    mine = lax.dynamic_index_in_dim(part, core, 0, keepdims=False)
    other = lax.dynamic_index_in_dim(part, 1 - core, 0, keepdims=False)
    got = lax.ppermute(other, "c", [(0, 1), (1, 0)])
    part = (mine + got).reshape(nx * ny, own * nz, cols)
    part = lax.all_to_all(part, ("x", "y"), 0, 0, tiled=True).sum(0)
    part = part.reshape(own, nz, cols // 128, 128).transpose(1, 2, 0, 3)
    part = part.reshape(nz, own * cols // 128, 128)
    part = lax.all_to_all(part, "z", 0, 0, tiled=True).sum(0)
    part = part.reshape(cols // 128, own, 128).transpose(1, 0, 2)
    return part.reshape(own, cols)


def per_device(diag_even, inv_odd, coupling, arrow_blocks, arrow_tip):
    half_count = inv_odd.shape[0]
    order = coupling.shape[1]
    width = arrow_blocks.shape[1]
    linked = coupling.reshape(half_count, 2, order, order)
    link_prev = linked[:, 0]
    link_next = linked[:, 1]
    paired = arrow_blocks.reshape(half_count, 2, width, order)
    arrow_even = paired[:, 0]
    arrow_odd = paired[:, 1]
    arrow_inv = product(arrow_odd, inv_odd)
    tip_part = jnp.einsum("hab,hcb->ac", arrow_inv, arrow_odd, precision=lax.Precision.HIGHEST)
    left_prod = product(link_prev, inv_odd)
    diag_left = product(left_prod, jnp.swapaxes(link_prev, 1, 2))
    couple_new = -product(left_prod, link_next)
    arrow_left = product(arrow_inv, jnp.swapaxes(link_prev, 1, 2))
    inv_next = product(inv_odd, link_next)
    diag_right = product(jnp.swapaxes(link_next, 1, 2), inv_next)
    arrow_right = product(arrow_odd, inv_next)
    sent = jnp.concatenate([diag_right[-1], arrow_right[-1]], axis=0)
    received = shifted(sent, 1)
    diag_shift = jnp.concatenate([received[None, :order], diag_right[:-1]], axis=0)
    arrow_shift = jnp.concatenate([received[None, order:], arrow_right[:-1]], axis=0)
    tip_new = arrow_tip - scattered_sum(tip_part)
    diag_new = diag_even - diag_left - diag_shift
    arrow_new = arrow_even - arrow_left - arrow_shift
    return (diag_new, couple_new, arrow_new, tip_new)


def solution(mesh):
    torus = Mesh(mesh.devices.reshape(SIZES), AXES)
    cube = P(AXES, None, None)
    flat = P(AXES, None)
    return jax.shard_map(
        per_device,
        mesh=torus,
        in_specs=(cube, cube, cube, cube, flat),
        out_specs=(cube, cube, cube, flat),
        check_vma=False,
    )
```

```python
import functools

import jax
import jax.numpy as jnp
from jax import lax
from jax.experimental import pallas as pl
from jax.experimental.pallas import tpu as pltpu
from jax.sharding import Mesh
from jax.sharding import PartitionSpec as P

AXES = ("x", "z", "y", "c")
SIZES = (4, 8, 4, 2)
F32 = jnp.float32
NN = (((1,), (0,)), ((), ()))
NT = (((1,), (1,)), ((), ()))
TN = (((0,), (0,)), ((), ()))
HBM = pl.BlockSpec(memory_space=pltpu.HBM)


def halves(x):
    high = x.astype(jnp.bfloat16)
    return high, (x - high.astype(F32)).astype(jnp.bfloat16)


def mul(a, b, dims):
    dot = functools.partial(lax.dot_general, dimension_numbers=dims, preferred_element_type=F32)
    return dot(a[0], b[0]) + (dot(a[0], b[1]) + dot(a[1], b[0]))


def start_all(pairs, sems):
    copies = [pltpu.make_async_copy(src, dst, sems.at[i]) for i, (src, dst) in enumerate(pairs)]
    for copy in copies:
        copy.start()
    return copies


def tip_kernel(inv_ref, arrow_ref, mine_ref, other_ref, p_buf, k_buf, a_buf, sems):
    nx, nz, ny, nc = SIZES
    copies = start_all(
        [pair for h in range(2) for pair in ((inv_ref.at[h], p_buf.at[h]), (arrow_ref.at[2 * h + 1], k_buf.at[h]))],
        sems,
    )
    rows = k_buf.shape[1]
    own = rows // (nx * nz * ny * nc)
    k_split = []
    for h in range(2):
        copies[2 * h].wait()
        copies[2 * h + 1].wait()
        k_split.append(halves(k_buf[h]))
        a = mul(k_split[h], halves(p_buf[h]), NN)
        a_buf[h, 0] = a[:, :128]
        a_buf[h, 1] = a[:, 128:]
    core = lax.axis_index("c")
    for out_ref, part in ((other_ref, 1 - core), (mine_ref, core)):
        total = None
        for h in range(2):
            tiles = []
            for x in range(nx):
                for y in range(ny):
                    for r in range(own):
                        first = ((x * nz * ny + y) * nc + part) * own + r
                        picked = pl.ds(first, nz, stride=ny * nc * own)
                        tiles.append(jnp.concatenate([a_buf[h, 0, picked, :], a_buf[h, 1, picked, :]], axis=1))
            a = halves(jnp.concatenate(tiles, axis=0))
            term = mul(a, k_split[h], NT)
            total = term if total is None else total + term
        out_ref[...] = total


def tip_parts(inv_odd, arrow_blocks):
    _, order, _ = inv_odd.shape
    width = arrow_blocks.shape[1]
    half = jax.ShapeDtypeStruct((width // 2, width), F32)
    return pl.pallas_call(
        tip_kernel,
        name="tip",
        out_shape=(half, half),
        in_specs=[HBM, HBM],
        scratch_shapes=[
            pltpu.VMEM((2, order, order), F32),
            pltpu.VMEM((2, width, order), F32),
            pltpu.VMEM((2, 2, width, order // 2), F32),
            pltpu.SemaphoreType.DMA((4,)),
        ],
        cost_estimate=pl.CostEstimate(flops=1_200_000_000, bytes_accessed=2_600_000, transcendentals=0),
        compiler_params=pltpu.CompilerParams(vmem_limit_bytes=24 << 20),
    )(inv_odd, arrow_blocks)


def right_kernel(inv_ref, link_ref, arrow_ref, sent_ref, p_buf, v_buf, k_buf, sems):
    copies = start_all([(inv_ref.at[1], p_buf), (link_ref.at[3], v_buf), (arrow_ref.at[3], k_buf)], sems)
    copies[0].wait()
    copies[1].wait()
    v = halves(v_buf[...])
    w = halves(mul(halves(p_buf[...]), v, NN))
    order = v_buf.shape[0]
    sent_ref[:order] = mul(v, w, TN)
    copies[2].wait()
    sent_ref[order:] = mul(halves(k_buf[...]), w, NN)


def right_parts(inv_odd, coupling, arrow_blocks):
    _, order, _ = inv_odd.shape
    width = arrow_blocks.shape[1]
    return pl.pallas_call(
        right_kernel,
        name="right",
        out_shape=jax.ShapeDtypeStruct((order + width, order), F32),
        in_specs=[HBM, HBM, HBM],
        scratch_shapes=[
            pltpu.VMEM((order, order), F32),
            pltpu.VMEM((order, order), F32),
            pltpu.VMEM((width, order), F32),
            pltpu.SemaphoreType.DMA((3,)),
        ],
        cost_estimate=pl.CostEstimate(flops=400_000_000, bytes_accessed=1_800_000, transcendentals=0),
        compiler_params=pltpu.CompilerParams(vmem_limit_bytes=24 << 20),
    )(inv_odd, coupling, arrow_blocks)


def rest_kernel(
    even_ref, inv_ref, link_ref, arrow_ref, diag_ref, couple_ref, new_ref,
    e_buf, p_buf, l_buf, k_buf, d_out, c_out, a_out, in_sems, out_sems,
):
    copies = start_all(
        [
            (inv_ref, p_buf),
            (link_ref, l_buf),
            (arrow_ref.at[1], k_buf.at[1]),
            (even_ref, e_buf),
            (arrow_ref.at[0], k_buf.at[0]),
            (arrow_ref.at[3], k_buf.at[3]),
            (arrow_ref.at[2], k_buf.at[2]),
        ],
        in_sems,
    )
    outs = []

    def send(src, dst):
        copy = pltpu.make_async_copy(src, dst, out_sems.at[len(outs)])
        copy.start()
        outs.append(copy)

    copies[0].wait()
    copies[1].wait()
    w = None
    for h in range(2):
        p, u, v = halves(p_buf[h]), halves(l_buf[2 * h]), halves(l_buf[2 * h + 1])
        left = halves(mul(u, p, NN))
        c_out[h] = -mul(left, v, NN)
        send(c_out.at[h], couple_ref.at[h])
        if h == 0:
            copies[2].wait()
            copies[3].wait()
        diag = e_buf[h] - mul(left, u, NT)
        k = halves(k_buf[1]) if h == 0 else None
        if h == 1:
            diag = diag - mul(v0, w, TN)
        d_out[h] = diag
        send(d_out.at[h], diag_ref.at[h])
        if h == 0:
            v0, k0 = v, k
            w = halves(mul(p, v, NN))
            copies[4].wait()
            a_out[0] = k_buf[0] - mul(k, left, NT)
        else:
            copies[5].wait()
            copies[6].wait()
            a_out[1] = k_buf[2] - mul(halves(k_buf[3]), left, NT) - mul(k0, w, NN)
        send(a_out.at[h], new_ref.at[h])
    for copy in outs:
        copy.wait()


def rest_parts(diag_even, inv_odd, coupling, arrow_blocks):
    half, order, _ = inv_odd.shape
    width = arrow_blocks.shape[1]
    square = jax.ShapeDtypeStruct((half, order, order), F32)
    tall = jax.ShapeDtypeStruct((half, width, order), F32)
    return pl.pallas_call(
        rest_kernel,
        name="rest",
        out_shape=(square, square, tall),
        in_specs=[HBM] * 4,
        out_specs=[HBM] * 3,
        scratch_shapes=[
            pltpu.VMEM((half, order, order), F32),
            pltpu.VMEM((half, order, order), F32),
            pltpu.VMEM((2 * half, order, order), F32),
            pltpu.VMEM((2 * half, width, order), F32),
            pltpu.VMEM((half, order, order), F32),
            pltpu.VMEM((half, order, order), F32),
            pltpu.VMEM((half, width, order), F32),
            pltpu.SemaphoreType.DMA((7,)),
            pltpu.SemaphoreType.DMA((6,)),
        ],
        cost_estimate=pl.CostEstimate(flops=1_400_000_000, bytes_accessed=6_000_000, transcendentals=0),
        compiler_params=pltpu.CompilerParams(vmem_limit_bytes=32 << 20),
    )(diag_even, inv_odd, coupling, arrow_blocks)


def settle_kernel(diag_ref, new_ref, got_ref, diag_out, new_out, d_buf, a_buf, g_buf, sems):
    order = d_buf.shape[0]
    copies = start_all([(diag_ref.at[0], d_buf), (got_ref, g_buf), (new_ref.at[0], a_buf)], sems)
    copies[0].wait()
    copies[1].wait()
    d_buf[...] = d_buf[...] - g_buf[:order]
    first = pltpu.make_async_copy(d_buf, diag_out.at[0], sems.at[0])
    first.start()
    copies[2].wait()
    a_buf[...] = a_buf[...] - g_buf[order:]
    second = pltpu.make_async_copy(a_buf, new_out.at[0], sems.at[1])
    second.start()
    first.wait()
    second.wait()


def settle(diag_part, arrow_part, received):
    _, order, _ = diag_part.shape
    width = arrow_part.shape[1]
    return pl.pallas_call(
        settle_kernel,
        name="settle",
        out_shape=(
            jax.ShapeDtypeStruct(diag_part.shape, F32),
            jax.ShapeDtypeStruct(arrow_part.shape, F32),
        ),
        in_specs=[HBM] * 3,
        out_specs=[HBM] * 2,
        input_output_aliases={0: 0, 1: 1},
        scratch_shapes=[
            pltpu.VMEM((order, order), F32),
            pltpu.VMEM((width, order), F32),
            pltpu.VMEM((order + width, order), F32),
            pltpu.SemaphoreType.DMA((3,)),
        ],
        cost_estimate=pl.CostEstimate(flops=200_000, bytes_accessed=2_400_000, transcendentals=0),
        compiler_params=pltpu.CompilerParams(vmem_limit_bytes=16 << 20),
    )(diag_part, arrow_part, received)


def shifted(x, by):
    count = 1
    for size in SIZES:
        count *= size
    pairs = [(i, i + by) for i in range(count) if 0 <= i + by < count]
    return lax.ppermute(x, AXES, pairs)


def per_device(diag_even, inv_odd, coupling, arrow_blocks, arrow_tip):
    own, cols = arrow_tip.shape
    nx, nz, ny, _ = SIZES
    diag_even, inv_odd, coupling, arrow_blocks = (
        pltpu.with_memory_space_constraint(x, pltpu.HBM) for x in (diag_even, inv_odd, coupling, arrow_blocks)
    )
    mine, other = tip_parts(inv_odd, arrow_blocks)
    got = lax.ppermute(other, "c", [(0, 1), (1, 0)])
    sent = right_parts(inv_odd, coupling, arrow_blocks)
    part = (mine + got).reshape(nx * ny, own * nz, cols)
    part = lax.all_to_all(part, ("x", "y"), 0, 0, tiled=True)
    part = part.sum(0)
    received = shifted(sent, 1)
    diag_part, couple_new, arrow_part = rest_parts(diag_even, inv_odd, coupling, arrow_blocks)
    part = part.reshape(own, nz, cols // 128, 128).transpose(1, 2, 0, 3)
    part = part.reshape(nz, own * cols // 128, 128)
    part = lax.all_to_all(part, "z", 0, 0, tiled=True)
    part = part.sum(0)
    part = part.reshape(cols // 128, own, 128).transpose(1, 0, 2)
    tip_new = arrow_tip - part.reshape(own, cols)
    diag_new, arrow_new = settle(diag_part, arrow_part, received)
    return (diag_new, couple_new, arrow_new, tip_new)


def solution(mesh):
    torus = Mesh(mesh.devices.reshape(SIZES), AXES)
    cube = P(AXES, None, None)
    flat = P(AXES, None)

    return jax.shard_map(
        per_device,
        mesh=torus,
        in_specs=(cube, cube, cube, cube, flat),
        out_specs=(cube, cube, cube, flat),
        check_vma=False,
    )
```

```python
import functools

import jax
import jax.numpy as jnp
from jax import lax
from jax.experimental import pallas as pl
from jax.experimental.pallas import tpu as pltpu
from jax.sharding import Mesh
from jax.sharding import PartitionSpec as P

AXES = ("x", "z", "y", "c")
SIZES = (4, 8, 4, 2)
F32 = jnp.float32
NN = (((1,), (0,)), ((), ()))
NT = (((1,), (1,)), ((), ()))
TN = (((0,), (0,)), ((), ()))
HBM = pl.BlockSpec(memory_space=pltpu.HBM)


def halves(x):
    high = x.astype(jnp.bfloat16)
    return high, (x - high.astype(F32)).astype(jnp.bfloat16)


def mul(a, b, dims):
    dot = functools.partial(lax.dot_general, dimension_numbers=dims, preferred_element_type=F32)
    return dot(a[0], b[0]) + (dot(a[0], b[1]) + dot(a[1], b[0]))


def start_all(pairs, sems):
    copies = [pltpu.make_async_copy(src, dst, sems.at[i]) for i, (src, dst) in enumerate(pairs)]
    for copy in copies:
        copy.start()
    return copies


def picked_rows(a_buf, h, part):
    nx, nz, ny, nc = SIZES
    own = a_buf.shape[2] // (nx * nz * ny * nc)
    tiles = []
    for x in range(nx):
        for y in range(ny):
            for r in range(own):
                first = ((x * nz * ny + y) * nc + part) * own + r
                rows = pl.ds(first, nz, stride=ny * nc * own)
                tiles.append(jnp.concatenate([a_buf[h, 0, rows, :], a_buf[h, 1, rows, :]], axis=1))
    return halves(jnp.concatenate(tiles, axis=0))


def tip_kernel(inv_ref, arrow_ref, other_ref, a_ref, k_ref, p_buf, k_buf, a_buf, sems):
    copies = start_all(
        [pair for h in range(2) for pair in ((inv_ref.at[h], p_buf.at[h]), (arrow_ref.at[2 * h + 1], k_buf.at[h]))],
        sems,
    )
    core = lax.axis_index("c")
    total = None
    for h in range(2):
        copies[2 * h].wait()
        copies[2 * h + 1].wait()
        k = halves(k_buf[h])
        k_ref[h, 0], k_ref[h, 1] = k
        a = mul(k, halves(p_buf[h]), NN)
        a_buf[h, 0] = a[:, :128]
        a_buf[h, 1] = a[:, 128:]
        term = mul(picked_rows(a_buf, h, 1 - core), k, NT)
        total = term if total is None else total + term
    other_ref[...] = total
    for h in range(2):
        a_ref[h, 0], a_ref[h, 1] = picked_rows(a_buf, h, core)


def tip_parts(inv_odd, arrow_blocks):
    half, order, _ = inv_odd.shape
    width = arrow_blocks.shape[1]
    return pl.pallas_call(
        tip_kernel,
        name="tip",
        out_shape=(
            jax.ShapeDtypeStruct((width // 2, width), F32),
            jax.ShapeDtypeStruct((half, 2, width // 2, order), jnp.bfloat16),
            jax.ShapeDtypeStruct((half, 2, width, order), jnp.bfloat16),
        ),
        in_specs=[HBM, HBM],
        scratch_shapes=[
            pltpu.VMEM((half, order, order), F32),
            pltpu.VMEM((half, width, order), F32),
            pltpu.VMEM((half, 2, width, order // 2), F32),
            pltpu.SemaphoreType.DMA((4,)),
        ],
        cost_estimate=pl.CostEstimate(flops=800_000_000, bytes_accessed=1_600_000, transcendentals=0),
        compiler_params=pltpu.CompilerParams(vmem_limit_bytes=24 << 20),
    )(inv_odd, arrow_blocks)


def mine_kernel(a_ref, k_ref, out_ref):
    terms = [mul((a_ref[h, 0], a_ref[h, 1]), (k_ref[h, 0], k_ref[h, 1]), NT) for h in range(2)]
    out_ref[...] = terms[0] + terms[1]


def mine_part(a_split, k_split):
    return pl.pallas_call(
        mine_kernel,
        name="mine",
        out_shape=jax.ShapeDtypeStruct((a_split.shape[2], k_split.shape[2]), F32),
        cost_estimate=pl.CostEstimate(flops=400_000_000, bytes_accessed=100_000, transcendentals=0),
        compiler_params=pltpu.CompilerParams(vmem_limit_bytes=24 << 20),
    )(a_split, k_split)


def add_kernel(a_ref, b_ref, out_ref):
    out_ref[...] = (a_ref[...] + b_ref[...]).reshape(out_ref.shape)


def added(a, b, shape):
    return pl.pallas_call(
        add_kernel,
        name="added",
        out_shape=jax.ShapeDtypeStruct(shape, F32),
        cost_estimate=pl.CostEstimate(flops=200_000, bytes_accessed=100_000, transcendentals=0),
        compiler_params=pltpu.CompilerParams(vmem_limit_bytes=16 << 20),
    )(a, b)


def fold_kernel(in_ref, out_ref):
    nz, deep, lanes = out_ref.shape
    own = in_ref.shape[1] // nz
    total = in_ref[0]
    for peer in range(1, in_ref.shape[0]):
        total = total + in_ref[peer]
    for block in range(deep // own):
        for r in range(own):
            piece = total[r * nz : (r + 1) * nz, block * lanes : (block + 1) * lanes]
            out_ref[:, block * own + r, :] = piece


def folded(part, own, nz):
    deep = own * part.shape[2] // 128
    return pl.pallas_call(
        fold_kernel,
        name="folded",
        out_shape=jax.ShapeDtypeStruct((nz, deep, 128), F32),
        cost_estimate=pl.CostEstimate(flops=200_000, bytes_accessed=100_000, transcendentals=0),
        compiler_params=pltpu.CompilerParams(vmem_limit_bytes=16 << 20),
    )(part)


def rest_kernel(
    even_ref, inv_ref, link_ref, arrow_ref, diag_ref, couple_ref, new_ref, sent_ref, held_ref,
    e_buf, p_buf, l_buf, k_buf, d_out, c_out, a_out, in_sems, out_sems,
):
    order = p_buf.shape[1]
    copies = start_all(
        [
            (inv_ref, p_buf),
            (link_ref, l_buf),
            (arrow_ref.at[3], k_buf.at[3]),
            (arrow_ref.at[1], k_buf.at[1]),
            (even_ref, e_buf),
            (arrow_ref.at[2], k_buf.at[2]),
            (arrow_ref.at[0], k_buf.at[0]),
        ],
        in_sems,
    )
    outs = []

    def send(src, dst):
        copy = pltpu.make_async_copy(src, dst, out_sems.at[len(outs)])
        copy.start()
        outs.append(copy)

    copies[0].wait()
    copies[1].wait()
    p = [halves(p_buf[h]) for h in range(2)]
    u = [halves(l_buf[2 * h]) for h in range(2)]
    v = [halves(l_buf[2 * h + 1]) for h in range(2)]
    left = []
    for h in range(2):
        left.append(halves(mul(u[h], p[h], NN)))
        c_out[h] = -mul(left[h], v[h], NN)
        send(c_out.at[h], couple_ref.at[h])
    w = [halves(mul(p[h], v[h], NN)) for h in range(2)]
    sent_ref[:order] = mul(v[1], w[1], TN)
    copies[2].wait()
    k = halves(k_buf[3])
    sent_ref[order:] = mul(k, w[1], NN)
    later = mul(k, left[1], NT)
    copies[4].wait()
    d_out[...] = e_buf[1] - mul(left[1], u[1], NT) - mul(v[0], w[0], TN)
    send(d_out, diag_ref.at[1])
    held_ref[:order] = e_buf[0] - mul(left[0], u[0], NT)
    copies[3].wait()
    k = halves(k_buf[1])
    copies[5].wait()
    a_out[...] = k_buf[2] - later - mul(k, w[0], NN)
    send(a_out, new_ref.at[1])
    copies[6].wait()
    held_ref[order:] = k_buf[0] - mul(k, left[0], NT)
    for copy in outs:
        copy.wait()


def rest_parts(diag_even, inv_odd, coupling, arrow_blocks):
    half, order, _ = inv_odd.shape
    width = arrow_blocks.shape[1]
    square = jax.ShapeDtypeStruct((half, order, order), F32)
    tall = jax.ShapeDtypeStruct((half, width, order), F32)
    tower = jax.ShapeDtypeStruct((order + width, order), F32)
    return pl.pallas_call(
        rest_kernel,
        name="rest",
        out_shape=(square, square, tall, tower, tower),
        in_specs=[HBM] * 4,
        out_specs=[HBM] * 3 + [pl.BlockSpec(memory_space=pltpu.VMEM)] * 2,
        scratch_shapes=[
            pltpu.VMEM((half, order, order), F32),
            pltpu.VMEM((half, order, order), F32),
            pltpu.VMEM((2 * half, order, order), F32),
            pltpu.VMEM((2 * half, width, order), F32),
            pltpu.VMEM((order, order), F32),
            pltpu.VMEM((half, order, order), F32),
            pltpu.VMEM((width, order), F32),
            pltpu.SemaphoreType.DMA((7,)),
            pltpu.SemaphoreType.DMA((4,)),
        ],
        cost_estimate=pl.CostEstimate(flops=1_800_000_000, bytes_accessed=6_000_000, transcendentals=0),
        compiler_params=pltpu.CompilerParams(vmem_limit_bytes=32 << 20),
    )(diag_even, inv_odd, coupling, arrow_blocks)


def settle_kernel(diag_ref, new_ref, held_ref, got_ref, diag_out, new_out, buf, sems):
    del diag_ref, new_ref
    order = got_ref.shape[1]
    buf[:order] = held_ref[:order] - got_ref[:order]
    first = pltpu.make_async_copy(buf.at[pl.ds(0, order)], diag_out.at[0], sems.at[0])
    first.start()
    buf[order:] = held_ref[order:] - got_ref[order:]
    second = pltpu.make_async_copy(buf.at[pl.ds(order, buf.shape[0] - order)], new_out.at[0], sems.at[1])
    second.start()
    first.wait()
    second.wait()


def settle(diag_part, arrow_part, held, received):
    return pl.pallas_call(
        settle_kernel,
        name="settle",
        out_shape=(
            jax.ShapeDtypeStruct(diag_part.shape, F32),
            jax.ShapeDtypeStruct(arrow_part.shape, F32),
        ),
        in_specs=[HBM] * 2 + [pl.BlockSpec(memory_space=pltpu.VMEM)] * 2,
        out_specs=[HBM] * 2,
        input_output_aliases={0: 0, 1: 1},
        scratch_shapes=[pltpu.VMEM(held.shape, F32), pltpu.SemaphoreType.DMA((2,))],
        cost_estimate=pl.CostEstimate(flops=200_000, bytes_accessed=1_000_000, transcendentals=0),
        compiler_params=pltpu.CompilerParams(vmem_limit_bytes=16 << 20),
    )(diag_part, arrow_part, held, received)


def shifted(x, by):
    count = 1
    for size in SIZES:
        count *= size
    pairs = [(i, i + by) for i in range(count) if 0 <= i + by < count]
    return lax.ppermute(x, AXES, pairs)


def per_device(diag_even, inv_odd, coupling, arrow_blocks, arrow_tip):
    own, cols = arrow_tip.shape
    nx, nz, ny, _ = SIZES
    diag_even, inv_odd, coupling, arrow_blocks = (
        pltpu.with_memory_space_constraint(x, pltpu.HBM) for x in (diag_even, inv_odd, coupling, arrow_blocks)
    )
    other, a_split, k_split = tip_parts(inv_odd, arrow_blocks)
    got = lax.ppermute(other, "c", [(0, 1), (1, 0)])
    mine = mine_part(a_split, k_split)
    part = added(mine, got, (nx * ny, own * nz, cols))
    part = lax.all_to_all(part, ("x", "y"), 0, 0, tiled=True)
    diag_part, couple_new, arrow_part, sent, held = rest_parts(diag_even, inv_odd, coupling, arrow_blocks)
    received = shifted(sent, 1)
    part = folded(part, own, nz)
    part = lax.all_to_all(part, "z", 0, 0, tiled=True)
    part = part.sum(0)
    part = part.reshape(cols // 128, own, 128).transpose(1, 0, 2)
    tip_new = arrow_tip - part.reshape(own, cols)
    diag_new, arrow_new = settle(diag_part, arrow_part, held, received)
    return (diag_new, couple_new, arrow_new, tip_new)


def solution(mesh):
    torus = Mesh(mesh.devices.reshape(SIZES), AXES)
    cube = P(AXES, None, None)
    flat = P(AXES, None)

    return jax.shard_map(
        per_device,
        mesh=torus,
        in_specs=(cube, cube, cube, cube, flat),
        out_specs=(cube, cube, cube, flat),
        check_vma=False,
    )
```

```python
import functools

import jax
import jax.numpy as jnp
from jax import lax
from jax.experimental import pallas as pl
from jax.experimental.pallas import tpu as pltpu
from jax.sharding import Mesh
from jax.sharding import PartitionSpec as P

AXES = ("x", "z", "y", "c")
SIZES = (4, 8, 4, 2)
PLANE = (
    (7, 1, 15, 6, 13, 4, 3, 5, 0, 8, 12, 11, 10, 9, 14, 2),
    (10, 15, 8, 3, 5, 14, 4, 9, 13, 1, 0, 2, 7, 6, 11, 12),
)
COLUMN = (4, 0, 2, 6, 1, 5, 3, 7)
F32 = jnp.float32
NN = (((1,), (0,)), ((), ()))
NT = (((1,), (1,)), ((), ()))
TN = (((0,), (0,)), ((), ()))
HBM = pl.BlockSpec(memory_space=pltpu.HBM)


def halves(x):
    high = x.astype(jnp.bfloat16)
    return high, (x - high.astype(F32)).astype(jnp.bfloat16)


def mul(a, b, dims):
    dot = functools.partial(lax.dot_general, dimension_numbers=dims, preferred_element_type=F32)
    return dot(a[0], b[0]) + (dot(a[0], b[1]) + dot(a[1], b[0]))


def start_all(pairs, sems):
    copies = [pltpu.make_async_copy(src, dst, sems.at[i]) for i, (src, dst) in enumerate(pairs)]
    for copy in copies:
        copy.start()
    return copies


def picked_rows(a_buf, h, part):
    nx, nz, ny, nc = SIZES
    own = a_buf.shape[2] // (nx * nz * ny * nc)
    tiles = []
    for chips in zip(*PLANE, strict=True):
        starts = [(chip // ny * nz * ny + chip % ny) * nc * own for chip in chips]
        start = jnp.where(part == 0, starts[0], starts[1]) + part * own
        for r in range(own):
            rows = pl.ds(start + r, nz, stride=ny * nc * own)
            tiles.append(jnp.concatenate([a_buf[h, 0, rows, :], a_buf[h, 1, rows, :]], axis=1))
    return halves(jnp.concatenate(tiles, axis=0))


def tip_kernel(inv_ref, arrow_ref, other_ref, a_ref, k_ref, p_ref, sems):
    copies = start_all(
        [pair for h in range(2) for pair in ((inv_ref.at[h], p_ref.at[h]), (arrow_ref.at[2 * h + 1], k_ref.at[h]))],
        sems,
    )
    core = lax.axis_index("c")
    total = None
    for h in range(2):
        copies[2 * h].wait()
        copies[2 * h + 1].wait()
        k = halves(k_ref[h])
        a = mul(k, halves(p_ref[h]), NN)
        a_ref[h, 0] = a[:, :128]
        a_ref[h, 1] = a[:, 128:]
        term = mul(picked_rows(a_ref, h, 1 - core), k, NT)
        total = term if total is None else total + term
    other_ref[...] = total


def tip_parts(inv_odd, arrow_blocks):
    half, order, _ = inv_odd.shape
    width = arrow_blocks.shape[1]
    return pl.pallas_call(
        tip_kernel,
        name="tip",
        out_shape=(
            jax.ShapeDtypeStruct((width // 2, width), F32),
            jax.ShapeDtypeStruct((half, 2, width, order // 2), F32),
            jax.ShapeDtypeStruct((half, width, order), F32),
            jax.ShapeDtypeStruct((half, order, order), F32),
        ),
        in_specs=[HBM, HBM],
        scratch_shapes=[pltpu.SemaphoreType.DMA((4,))],
        cost_estimate=pl.CostEstimate(flops=800_000_000, bytes_accessed=1_600_000, transcendentals=0),
        compiler_params=pltpu.CompilerParams(vmem_limit_bytes=24 << 20),
    )(inv_odd, arrow_blocks)


def mine_kernel(a_ref, k_ref, p_ref, link_ref, out_ref, sent_ref, v_buf, sem):
    copy = pltpu.make_async_copy(link_ref.at[3], v_buf, sem)
    copy.start()
    core = lax.axis_index("c")
    k = [halves(k_ref[h]) for h in range(2)]
    out_ref[...] = mul(picked_rows(a_ref, 0, core), k[0], NT) + mul(picked_rows(a_ref, 1, core), k[1], NT)
    copy.wait()
    order = v_buf.shape[0]
    v = halves(v_buf[...])
    w = halves(mul(halves(p_ref[1]), v, NN))
    sent_ref[:order] = mul(v, w, TN)
    sent_ref[order:] = mul(k[1], w, NN)


def mine_part(a, k, p, coupling):
    _, width, order = k.shape
    vmem = pl.BlockSpec(memory_space=pltpu.VMEM)
    return pl.pallas_call(
        mine_kernel,
        name="mine",
        out_shape=(
            jax.ShapeDtypeStruct((width // 2, width), F32),
            jax.ShapeDtypeStruct((order + width, order), F32),
        ),
        in_specs=[vmem, vmem, vmem, HBM],
        scratch_shapes=[pltpu.VMEM((order, order), F32), pltpu.SemaphoreType.DMA(())],
        cost_estimate=pl.CostEstimate(flops=800_000_000, bytes_accessed=300_000, transcendentals=0),
        compiler_params=pltpu.CompilerParams(vmem_limit_bytes=24 << 20),
    )(a, k, p, coupling)


def add_kernel(a_ref, b_ref, out_ref, buf, sems):
    pieces = sems.shape[0]
    rows = a_ref.shape[0] // pieces
    copies = []
    for i in range(pieces):
        part = slice(i * rows, (i + 1) * rows)
        major = pl.ds(i * buf.shape[0] // pieces, buf.shape[0] // pieces)
        buf[major] = (a_ref[part] + b_ref[part]).reshape(buf.shape[0] // pieces, *buf.shape[1:])
        copies.append(pltpu.make_async_copy(buf.at[major], out_ref.at[major], sems.at[i]))
        copies[-1].start()
    for copy in copies:
        copy.wait()


def added(a, b, shape):
    return pl.pallas_call(
        add_kernel,
        name="added",
        out_shape=jax.ShapeDtypeStruct(shape, F32),
        out_specs=HBM,
        scratch_shapes=[pltpu.VMEM(shape, F32), pltpu.SemaphoreType.DMA((4,))],
        cost_estimate=pl.CostEstimate(flops=200_000, bytes_accessed=100_000, transcendentals=0),
        compiler_params=pltpu.CompilerParams(vmem_limit_bytes=16 << 20),
    )(a, b)


def fold_kernel(in_ref, out_ref):
    nz, deep, lanes = out_ref.shape
    own = in_ref.shape[1] // nz
    total = in_ref[0]
    for peer in range(1, in_ref.shape[0]):
        total = total + in_ref[peer]
    for block in range(deep // own):
        for r in range(own):
            for k, z in enumerate(COLUMN):
                row = slice(r * nz + z, r * nz + z + 1)
                out_ref[k, block * own + r : block * own + r + 1, :] = total[row, block * lanes : (block + 1) * lanes]


def folded(part, own, nz):
    deep = own * part.shape[2] // 128
    return pl.pallas_call(
        fold_kernel,
        name="folded",
        out_shape=jax.ShapeDtypeStruct((nz, deep, 128), F32),
        cost_estimate=pl.CostEstimate(flops=200_000, bytes_accessed=100_000, transcendentals=0),
        compiler_params=pltpu.CompilerParams(vmem_limit_bytes=16 << 20),
    )(part)


def final_kernel(in_ref, tip_ref, out_ref):
    total = in_ref[0]
    for peer in range(1, in_ref.shape[0]):
        total = total + in_ref[peer]
    own, cols = out_ref.shape
    for block in range(cols // 128):
        lanes = slice(block * 128, (block + 1) * 128)
        out_ref[:, lanes] = tip_ref[:, lanes] - total[block * own : (block + 1) * own]


def final(part, arrow_tip):
    return pl.pallas_call(
        final_kernel,
        name="final",
        out_shape=jax.ShapeDtypeStruct(arrow_tip.shape, F32),
        cost_estimate=pl.CostEstimate(flops=10_000, bytes_accessed=40_000, transcendentals=0),
        compiler_params=pltpu.CompilerParams(vmem_limit_bytes=16 << 20),
    )(part, arrow_tip)


def send(src, dst, sem):
    copy = pltpu.make_async_copy(src, dst, sem)
    copy.start()
    return copy


def square_kernel(
    even_ref, inv_ref, link_ref, diag_ref, couple_ref, held_ref, left_ref, w_ref,
    e_buf, p_buf, l_buf, d_out, c_out, in_sems, out_sems,
):
    copies = start_all(
        [(inv_ref.at[0], p_buf.at[0]), (link_ref.at[pl.ds(0, 2)], l_buf.at[pl.ds(0, 2)])]
        + [(inv_ref.at[1], p_buf.at[1]), (link_ref.at[pl.ds(2, 2)], l_buf.at[pl.ds(2, 2)]), (even_ref, e_buf)],
        in_sems,
    )
    outs = []
    left, u, v = [], [], []
    for h in range(2):
        copies[2 * h].wait()
        copies[2 * h + 1].wait()
        p = halves(p_buf[h])
        u.append(halves(l_buf[2 * h]))
        v.append(halves(l_buf[2 * h + 1]))
        left.append(halves(mul(u[h], p, NN)))
        left_ref[h, 0], left_ref[h, 1] = left[h]
        c_out[h] = -mul(left[h], v[h], NN)
        outs.append(send(c_out.at[h], couple_ref.at[h], out_sems.at[h]))
        if h == 0:
            w = halves(mul(p, v[0], NN))
            w_ref[0], w_ref[1] = w
    copies[4].wait()
    d_out[...] = e_buf[1] - mul(left[1], u[1], NT) - mul(v[0], w, TN)
    outs.append(send(d_out, diag_ref.at[1], out_sems.at[2]))
    held_ref[...] = e_buf[0] - mul(left[0], u[0], NT)
    for copy in outs:
        copy.wait()


def square_parts(diag_even, inv_odd, coupling):
    half, order, _ = inv_odd.shape
    vmem = pl.BlockSpec(memory_space=pltpu.VMEM)
    blocks = jax.ShapeDtypeStruct((half, order, order), F32)
    pair = pltpu.VMEM((half, order, order), F32)
    return pl.pallas_call(
        square_kernel,
        name="square",
        out_shape=(
            blocks,
            blocks,
            jax.ShapeDtypeStruct((order, order), F32),
            jax.ShapeDtypeStruct((half, 2, order, order), jnp.bfloat16),
            jax.ShapeDtypeStruct((2, order, order), jnp.bfloat16),
        ),
        in_specs=[HBM] * 3,
        out_specs=[HBM, HBM, vmem, vmem, vmem],
        scratch_shapes=[
            pair,
            pair,
            pltpu.VMEM((2 * half, order, order), F32),
            pltpu.VMEM((order, order), F32),
            pair,
            pltpu.SemaphoreType.DMA((5,)),
            pltpu.SemaphoreType.DMA((3,)),
        ],
        cost_estimate=pl.CostEstimate(flops=800_000_000, bytes_accessed=2_700_000, transcendentals=0),
        compiler_params=pltpu.CompilerParams(vmem_limit_bytes=24 << 20),
    )(diag_even, inv_odd, coupling)


def tall_kernel(arrow_ref, left_ref, w_ref, new_ref, held_ref, k_buf, a_out, in_sems, out_sem):
    frames = (3, 1, 2, 0)
    copies = start_all([(arrow_ref.at[i], k_buf.at[i]) for i in frames], in_sems)
    copies[0].wait()
    later = mul(halves(k_buf[3]), (left_ref[1, 0], left_ref[1, 1]), NT)
    copies[1].wait()
    k = halves(k_buf[1])
    later = later + mul(k, (w_ref[0], w_ref[1]), NN)
    copies[2].wait()
    a_out[...] = k_buf[2] - later
    out = send(a_out, new_ref.at[1], out_sem)
    copies[3].wait()
    held_ref[...] = k_buf[0] - mul(k, (left_ref[0, 0], left_ref[0, 1]), NT)
    out.wait()


def tall_parts(arrow_blocks, left, w):
    frames, width, order = arrow_blocks.shape
    vmem = pl.BlockSpec(memory_space=pltpu.VMEM)
    return pl.pallas_call(
        tall_kernel,
        name="tall",
        out_shape=(
            jax.ShapeDtypeStruct((frames // 2, width, order), F32),
            jax.ShapeDtypeStruct((width, order), F32),
        ),
        in_specs=[HBM, vmem, vmem],
        out_specs=[HBM, vmem],
        scratch_shapes=[
            pltpu.VMEM((frames, width, order), F32),
            pltpu.VMEM((width, order), F32),
            pltpu.SemaphoreType.DMA((4,)),
            pltpu.SemaphoreType.DMA(()),
        ],
        cost_estimate=pl.CostEstimate(flops=600_000_000, bytes_accessed=2_600_000, transcendentals=0),
        compiler_params=pltpu.CompilerParams(vmem_limit_bytes=24 << 20),
    )(arrow_blocks, left, w)


def settle_kernel(diag_ref, new_ref, square_ref, tall_ref, got_ref, diag_out, new_out, d_buf, a_buf, sems):
    del diag_ref, new_ref
    order = got_ref.shape[1]
    d_buf[...] = square_ref[...] - got_ref[:order]
    first = send(d_buf, diag_out.at[0], sems.at[0])
    a_buf[...] = tall_ref[...] - got_ref[order:]
    second = send(a_buf, new_out.at[0], sems.at[1])
    first.wait()
    second.wait()


def settle(diag_part, arrow_part, square, tall, received):
    return pl.pallas_call(
        settle_kernel,
        name="settle",
        out_shape=(
            jax.ShapeDtypeStruct(diag_part.shape, F32),
            jax.ShapeDtypeStruct(arrow_part.shape, F32),
        ),
        in_specs=[HBM] * 2 + [pl.BlockSpec(memory_space=pltpu.VMEM)] * 3,
        out_specs=[HBM] * 2,
        input_output_aliases={0: 0, 1: 1},
        scratch_shapes=[
            pltpu.VMEM(square.shape, F32),
            pltpu.VMEM(tall.shape, F32),
            pltpu.SemaphoreType.DMA((2,)),
        ],
        cost_estimate=pl.CostEstimate(flops=200_000, bytes_accessed=1_000_000, transcendentals=0),
        compiler_params=pltpu.CompilerParams(vmem_limit_bytes=16 << 20),
    )(diag_part, arrow_part, square, tall, received)


def place(x, z, y, core):
    _, nz, ny, nc = SIZES
    return ((x * nz + z) * ny + y) * nc + core


def plane_groups():
    _, nz, ny, nc = SIZES
    return [[place(chip // ny, z, chip % ny, core) for chip in PLANE[core]] for z in range(nz) for core in range(nc)]


def column_groups():
    nx, _, ny, nc = SIZES
    return [[place(x, z, y, core) for z in COLUMN] for x in range(nx) for y in range(ny) for core in range(nc)]


def shifted(x, by):
    count = 1
    for size in SIZES:
        count *= size
    pairs = [(i, i + by) for i in range(count) if 0 <= i + by < count]
    return lax.ppermute(x, AXES, pairs)


def per_device(diag_even, inv_odd, coupling, arrow_blocks, arrow_tip):
    own, cols = arrow_tip.shape
    nx, nz, ny, _ = SIZES
    diag_even, inv_odd, coupling, arrow_blocks = (
        pltpu.with_memory_space_constraint(x, pltpu.HBM) for x in (diag_even, inv_odd, coupling, arrow_blocks)
    )
    other, a_kept, k_kept, p_kept = tip_parts(inv_odd, arrow_blocks)
    got = lax.ppermute(other, "c", [(0, 1), (1, 0)])
    mine, sent = mine_part(a_kept, k_kept, p_kept, coupling)
    part = added(mine, got, (nx * ny, own * nz, cols))
    part = lax.all_to_all(part, AXES, 0, 0, axis_index_groups=plane_groups(), tiled=True)
    diag_part, couple_new, square, left, w = square_parts(diag_even, inv_odd, coupling)
    received = shifted(sent, 1)
    arrow_part, tall = tall_parts(arrow_blocks, left, w)
    part = folded(part, own, nz)
    part = lax.all_to_all(part, AXES, 0, 0, axis_index_groups=column_groups(), tiled=True)
    tip_new = final(part, arrow_tip)
    diag_new, arrow_new = settle(diag_part, arrow_part, square, tall, received)
    return (diag_new, couple_new, arrow_new, tip_new)


def solution(mesh):
    torus = Mesh(mesh.devices.reshape(SIZES), AXES)
    cube = P(AXES, None, None)
    flat = P(AXES, None)

    return jax.shard_map(
        per_device,
        mesh=torus,
        in_specs=(cube, cube, cube, cube, flat),
        out_specs=(cube, cube, cube, flat),
        check_vma=False,
    )
```

```python
import functools

import jax
import jax.numpy as jnp
from jax import lax
from jax.experimental import pallas as pl
from jax.experimental.pallas import tpu as pltpu
from jax.sharding import Mesh
from jax.sharding import PartitionSpec as P

AXES = ("x", "z", "y", "c")
SIZES = (4, 8, 4, 2)
PLANE = (
    (7, 1, 15, 6, 13, 4, 3, 5, 0, 8, 12, 11, 10, 9, 14, 2),
    (10, 15, 8, 3, 5, 14, 4, 9, 13, 1, 0, 2, 7, 6, 11, 12),
)
COLUMN = (4, 0, 2, 6, 1, 5, 3, 7)
F32 = jnp.float32
NN = (((1,), (0,)), ((), ()))
NT = (((1,), (1,)), ((), ()))
TN = (((0,), (0,)), ((), ()))
HBM = pl.BlockSpec(memory_space=pltpu.HBM)
VMEM = pl.BlockSpec(memory_space=pltpu.VMEM)


def halves(x):
    high = x.astype(jnp.bfloat16)
    return high, (x - high.astype(F32)).astype(jnp.bfloat16)


def mul(a, b, dims):
    dot = functools.partial(lax.dot_general, dimension_numbers=dims, preferred_element_type=F32)
    return dot(a[0], b[0]) + (dot(a[0], b[1]) + dot(a[1], b[0]))


def start_all(pairs, sems):
    copies = [pltpu.make_async_copy(src, dst, sems.at[i]) for i, (src, dst) in enumerate(pairs)]
    for copy in copies:
        copy.start()
    return copies


def send(src, dst, sem):
    copy = pltpu.make_async_copy(src, dst, sem)
    copy.start()
    return copy


def picked_rows(a_buf, h, part):
    nx, nz, ny, nc = SIZES
    own = a_buf.shape[2] // (nx * nz * ny * nc)
    tiles = []
    for chips in zip(*PLANE, strict=True):
        starts = [(chip // ny * nz * ny + chip % ny) * nc * own for chip in chips]
        start = jnp.where(part == 0, starts[0], starts[1]) + part * own
        for r in range(own):
            rows = pl.ds(start + r, nz, stride=ny * nc * own)
            tiles.append(jnp.concatenate([a_buf[h, 0, rows, :], a_buf[h, 1, rows, :]], axis=1))
    return halves(jnp.concatenate(tiles, axis=0))


def tip_kernel(inv_ref, arrow_ref, other_ref, a_ref, k_ref, p_ref, sems):
    rows = k_ref.shape[1] // 2
    pieces = [pl.ds(0, rows), pl.ds(rows, rows)]
    pairs = []
    for h in range(2):
        pairs.append((inv_ref.at[h], p_ref.at[h]))
        pairs += [(arrow_ref.at[2 * h + 1, piece], k_ref.at[h, piece]) for piece in pieces]
    copies = start_all(pairs, sems)
    core = lax.axis_index("c")
    total = None
    for h in range(2):
        copies[3 * h].wait()
        p = halves(p_ref[h])
        parts = []
        for i, piece in enumerate(pieces):
            copies[3 * h + 1 + i].wait()
            parts.append(halves(k_ref[h, piece]))
            a = mul(parts[i], p, NN)
            a_ref[h, 0, piece] = a[:, :128]
            a_ref[h, 1, piece] = a[:, 128:]
        k = tuple(jnp.concatenate(both, axis=0) for both in zip(*parts, strict=True))
        term = mul(picked_rows(a_ref, h, 1 - core), k, NT)
        total = term if total is None else total + term
    other_ref[...] = total


def tip_parts(inv_odd, arrow_blocks):
    half, order, _ = inv_odd.shape
    width = arrow_blocks.shape[1]
    return pl.pallas_call(
        tip_kernel,
        name="tip",
        out_shape=(
            jax.ShapeDtypeStruct((width // 2, width), F32),
            jax.ShapeDtypeStruct((half, 2, width, order // 2), F32),
            jax.ShapeDtypeStruct((half, width, order), F32),
            jax.ShapeDtypeStruct((half, order, order), F32),
        ),
        in_specs=[HBM, HBM],
        scratch_shapes=[pltpu.SemaphoreType.DMA((6,))],
        cost_estimate=pl.CostEstimate(flops=800_000_000, bytes_accessed=1_600_000, transcendentals=0),
        compiler_params=pltpu.CompilerParams(vmem_limit_bytes=24 << 20),
    )(inv_odd, arrow_blocks)


def mine_kernel(a_ref, k_ref, link_in, out_ref, link_ref, sem):
    copy = send(link_in, link_ref, sem)
    core = lax.axis_index("c")
    terms = [mul(picked_rows(a_ref, h, core), halves(k_ref[h]), NT) for h in range(2)]
    out_ref[...] = terms[0] + terms[1]
    copy.wait()


def mine_part(a, k, coupling):
    _, width, _ = k.shape
    return pl.pallas_call(
        mine_kernel,
        name="mine",
        out_shape=(
            jax.ShapeDtypeStruct((width // 2, width), F32),
            jax.ShapeDtypeStruct(coupling.shape, F32),
        ),
        in_specs=[VMEM, VMEM, HBM],
        out_specs=[VMEM] * 2,
        scratch_shapes=[pltpu.SemaphoreType.DMA(())],
        cost_estimate=pl.CostEstimate(flops=400_000_000, bytes_accessed=1_500_000, transcendentals=0),
        compiler_params=pltpu.CompilerParams(vmem_limit_bytes=24 << 20),
    )(a, k, coupling)


def right_kernel(k_ref, p_ref, link_ref, sent_ref):
    order = p_ref.shape[1]
    v = halves(link_ref[3])
    w = halves(mul(halves(p_ref[1]), v, NN))
    sent_ref[:order] = mul(v, w, TN)
    sent_ref[order:] = mul(halves(k_ref[1]), w, NN)


def right_parts(k, p, link):
    _, width, order = k.shape
    return pl.pallas_call(
        right_kernel,
        name="right",
        out_shape=jax.ShapeDtypeStruct((order + width, order), F32),
        in_specs=[VMEM] * 3,
        out_specs=VMEM,
        cost_estimate=pl.CostEstimate(flops=400_000_000, bytes_accessed=100_000, transcendentals=0),
        compiler_params=pltpu.CompilerParams(vmem_limit_bytes=24 << 20),
    )(k, p, link)


def add_kernel(a_ref, b_ref, out_ref, buf, sems):
    pieces = sems.shape[0]
    rows = a_ref.shape[0] // pieces
    copies = []
    for i in range(pieces):
        part = slice(i * rows, (i + 1) * rows)
        major = pl.ds(i * buf.shape[0] // pieces, buf.shape[0] // pieces)
        buf[major] = (a_ref[part] + b_ref[part]).reshape(buf.shape[0] // pieces, *buf.shape[1:])
        copies.append(pltpu.make_async_copy(buf.at[major], out_ref.at[major], sems.at[i]))
        copies[-1].start()
    for copy in copies:
        copy.wait()


def added(a, b, shape):
    return pl.pallas_call(
        add_kernel,
        name="added",
        out_shape=jax.ShapeDtypeStruct(shape, F32),
        out_specs=HBM,
        scratch_shapes=[pltpu.VMEM(shape, F32), pltpu.SemaphoreType.DMA((4,))],
        cost_estimate=pl.CostEstimate(flops=200_000, bytes_accessed=100_000, transcendentals=0),
        compiler_params=pltpu.CompilerParams(vmem_limit_bytes=16 << 20),
    )(a, b)


def fold_kernel(in_ref, out_ref):
    nz, deep, lanes = out_ref.shape
    own = in_ref.shape[1] // nz
    total = in_ref[0]
    for peer in range(1, in_ref.shape[0]):
        total = total + in_ref[peer]
    for block in range(deep // own):
        for r in range(own):
            for k, z in enumerate(COLUMN):
                row = slice(r * nz + z, r * nz + z + 1)
                out_ref[k, block * own + r : block * own + r + 1, :] = total[row, block * lanes : (block + 1) * lanes]


def folded(part, own, nz):
    deep = own * part.shape[2] // 128
    return pl.pallas_call(
        fold_kernel,
        name="folded",
        out_shape=jax.ShapeDtypeStruct((nz, deep, 128), F32),
        cost_estimate=pl.CostEstimate(flops=200_000, bytes_accessed=100_000, transcendentals=0),
        compiler_params=pltpu.CompilerParams(vmem_limit_bytes=16 << 20),
    )(part)


def final_kernel(in_ref, tip_ref, out_ref):
    total = in_ref[0]
    for peer in range(1, in_ref.shape[0]):
        total = total + in_ref[peer]
    own, cols = out_ref.shape
    for block in range(cols // 128):
        lanes = slice(block * 128, (block + 1) * 128)
        out_ref[:, lanes] = tip_ref[:, lanes] - total[block * own : (block + 1) * own]


def final(part, arrow_tip):
    return pl.pallas_call(
        final_kernel,
        name="final",
        out_shape=jax.ShapeDtypeStruct(arrow_tip.shape, F32),
        cost_estimate=pl.CostEstimate(flops=10_000, bytes_accessed=40_000, transcendentals=0),
        compiler_params=pltpu.CompilerParams(vmem_limit_bytes=16 << 20),
    )(part, arrow_tip)


def square_kernel(
    even_in, p_ref, link_ref, arrow_in, diag_ref, couple_ref, held_ref, left_ref, w_ref, arrow_ref,
    even_ref, d_out, c_out, in_sems, out_sems,
):
    copies = start_all([(even_in, even_ref)] + [(arrow_in.at[2 * h], arrow_ref.at[h]) for h in range(2)], in_sems)
    outs = []
    left, u, v = [], [], []
    for h in range(2):
        p = halves(p_ref[h])
        u.append(halves(link_ref[2 * h]))
        v.append(halves(link_ref[2 * h + 1]))
        left.append(halves(mul(u[h], p, NN)))
        left_ref[h, 0], left_ref[h, 1] = left[h]
        c_out[h] = -mul(left[h], v[h], NN)
        outs.append(send(c_out.at[h], couple_ref.at[h], out_sems.at[h]))
        if h == 0:
            w = halves(mul(p, v[0], NN))
            w_ref[0], w_ref[1] = w
    copies[0].wait()
    d_out[...] = even_ref[1] - mul(left[1], u[1], NT) - mul(v[0], w, TN)
    outs.append(send(d_out, diag_ref.at[1], out_sems.at[2]))
    held_ref[...] = even_ref[0] - mul(left[0], u[0], NT)
    for copy in copies[1:] + outs:
        copy.wait()


def square_parts(even, p, link, arrow_blocks):
    half, order, _ = p.shape
    width = arrow_blocks.shape[1]
    blocks = jax.ShapeDtypeStruct((half, order, order), F32)
    return pl.pallas_call(
        square_kernel,
        name="square",
        out_shape=(
            blocks,
            blocks,
            jax.ShapeDtypeStruct((order, order), F32),
            jax.ShapeDtypeStruct((half, 2, order, order), jnp.bfloat16),
            jax.ShapeDtypeStruct((2, order, order), jnp.bfloat16),
            jax.ShapeDtypeStruct((half, width, order), F32),
        ),
        in_specs=[HBM, VMEM, VMEM, HBM],
        out_specs=[HBM, HBM] + [VMEM] * 4,
        scratch_shapes=[
            pltpu.VMEM((half, order, order), F32),
            pltpu.VMEM((order, order), F32),
            pltpu.VMEM((half, order, order), F32),
            pltpu.SemaphoreType.DMA((3,)),
            pltpu.SemaphoreType.DMA((3,)),
        ],
        cost_estimate=pl.CostEstimate(flops=800_000_000, bytes_accessed=1_700_000, transcendentals=0),
        compiler_params=pltpu.CompilerParams(vmem_limit_bytes=24 << 20),
    )(even, p, link, arrow_blocks)


def tall_kernel(arrow_ref, k_ref, left_ref, w_ref, new_ref, held_ref, a_out, sem):
    later = mul(halves(k_ref[1]), (left_ref[1, 0], left_ref[1, 1]), NT)
    k = halves(k_ref[0])
    a_out[...] = arrow_ref[1] - (later + mul(k, (w_ref[0], w_ref[1]), NN))
    out = send(a_out, new_ref.at[1], sem)
    held_ref[...] = arrow_ref[0] - mul(k, (left_ref[0, 0], left_ref[0, 1]), NT)
    out.wait()


def tall_parts(arrow_even, k, left, w):
    half, width, order = k.shape
    return pl.pallas_call(
        tall_kernel,
        name="tall",
        out_shape=(
            jax.ShapeDtypeStruct((half, width, order), F32),
            jax.ShapeDtypeStruct((width, order), F32),
        ),
        in_specs=[VMEM] * 4,
        out_specs=[HBM, VMEM],
        scratch_shapes=[pltpu.VMEM((width, order), F32), pltpu.SemaphoreType.DMA(())],
        cost_estimate=pl.CostEstimate(flops=600_000_000, bytes_accessed=600_000, transcendentals=0),
        compiler_params=pltpu.CompilerParams(vmem_limit_bytes=24 << 20),
    )(arrow_even, k, left, w)


def settle_kernel(diag_ref, new_ref, square_ref, tall_ref, got_ref, diag_out, new_out, d_buf, a_buf, sems):
    del diag_ref, new_ref
    order = got_ref.shape[1]
    d_buf[...] = square_ref[...] - got_ref[:order]
    first = send(d_buf, diag_out.at[0], sems.at[0])
    a_buf[...] = tall_ref[...] - got_ref[order:]
    second = send(a_buf, new_out.at[0], sems.at[1])
    first.wait()
    second.wait()


def settle(diag_part, arrow_part, square, tall, received):
    return pl.pallas_call(
        settle_kernel,
        name="settle",
        out_shape=(
            jax.ShapeDtypeStruct(diag_part.shape, F32),
            jax.ShapeDtypeStruct(arrow_part.shape, F32),
        ),
        in_specs=[HBM] * 2 + [VMEM] * 3,
        out_specs=[HBM] * 2,
        input_output_aliases={0: 0, 1: 1},
        scratch_shapes=[
            pltpu.VMEM(square.shape, F32),
            pltpu.VMEM(tall.shape, F32),
            pltpu.SemaphoreType.DMA((2,)),
        ],
        cost_estimate=pl.CostEstimate(flops=200_000, bytes_accessed=1_000_000, transcendentals=0),
        compiler_params=pltpu.CompilerParams(vmem_limit_bytes=16 << 20),
    )(diag_part, arrow_part, square, tall, received)


def place(x, z, y, core):
    _, nz, ny, nc = SIZES
    return ((x * nz + z) * ny + y) * nc + core


def plane_groups():
    _, nz, ny, nc = SIZES
    return [[place(chip // ny, z, chip % ny, core) for chip in PLANE[core]] for z in range(nz) for core in range(nc)]


def column_groups():
    nx, _, ny, nc = SIZES
    return [[place(x, z, y, core) for z in COLUMN] for x in range(nx) for y in range(ny) for core in range(nc)]


def shifted(x, by):
    count = 1
    for size in SIZES:
        count *= size
    pairs = [(i, i + by) for i in range(count) if 0 <= i + by < count]
    return lax.ppermute(x, AXES, pairs)


def per_device(diag_even, inv_odd, coupling, arrow_blocks, arrow_tip):
    own, cols = arrow_tip.shape
    nx, nz, ny, _ = SIZES
    diag_even, inv_odd, coupling, arrow_blocks = (
        pltpu.with_memory_space_constraint(x, pltpu.HBM) for x in (diag_even, inv_odd, coupling, arrow_blocks)
    )
    other, a_kept, k_kept, p_kept = tip_parts(inv_odd, arrow_blocks)
    got = lax.ppermute(other, "c", [(0, 1), (1, 0)])
    mine, link = mine_part(a_kept, k_kept, coupling)
    part = added(mine, got, (nx * ny, own * nz, cols))
    part = lax.all_to_all(part, AXES, 0, 0, axis_index_groups=plane_groups(), tiled=True)
    sent = right_parts(k_kept, p_kept, link)
    diag_part, couple_new, square, left, w, arrow_even = square_parts(diag_even, p_kept, link, arrow_blocks)
    received = shifted(sent, 1)
    arrow_part, tall = tall_parts(arrow_even, k_kept, left, w)
    part = folded(part, own, nz)
    part = lax.all_to_all(part, AXES, 0, 0, axis_index_groups=column_groups(), tiled=True)
    tip_new = final(part, arrow_tip)
    diag_new, arrow_new = settle(diag_part, arrow_part, square, tall, received)
    return (diag_new, couple_new, arrow_new, tip_new)


def solution(mesh):
    torus = Mesh(mesh.devices.reshape(SIZES), AXES)
    cube = P(AXES, None, None)
    flat = P(AXES, None)

    return jax.shard_map(
        per_device,
        mesh=torus,
        in_specs=(cube, cube, cube, cube, flat),
        out_specs=(cube, cube, cube, flat),
        check_vma=False,
    )
```

```python
import functools

import jax
import jax.numpy as jnp
from jax import lax
from jax.experimental import pallas as pl
from jax.experimental.pallas import tpu as pltpu
from jax.sharding import Mesh
from jax.sharding import PartitionSpec as P

AXES = ("x", "z", "y", "c")
SIZES = (4, 8, 4, 2)
PLANE = (
    (7, 1, 15, 6, 13, 4, 3, 5, 0, 8, 12, 11, 10, 9, 14, 2),
    (10, 15, 8, 3, 5, 14, 4, 9, 13, 1, 0, 2, 7, 6, 11, 12),
)
COLUMN = (4, 0, 2, 6, 1, 5, 3, 7)
F32 = jnp.float32
NN = (((1,), (0,)), ((), ()))
NT = (((1,), (1,)), ((), ()))
TN = (((0,), (0,)), ((), ()))
HBM = pl.BlockSpec(memory_space=pltpu.HBM)
VMEM = pl.BlockSpec(memory_space=pltpu.VMEM)


def halves(x):
    high = x.astype(jnp.bfloat16)
    return high, (x - high.astype(F32)).astype(jnp.bfloat16)


def mul(a, b, dims):
    dot = functools.partial(lax.dot_general, dimension_numbers=dims, preferred_element_type=F32)
    return dot(a[0], b[0]) + (dot(a[0], b[1]) + dot(a[1], b[0]))


def start_all(pairs, sems):
    copies = [pltpu.make_async_copy(src, dst, sems.at[i]) for i, (src, dst) in enumerate(pairs)]
    for copy in copies:
        copy.start()
    return copies


def send(src, dst, sem):
    copy = pltpu.make_async_copy(src, dst, sem)
    copy.start()
    return copy


def picked_rows(k_ref, h, part):
    nx, nz, ny, nc = SIZES
    own = k_ref.shape[2] // (nx * nz * ny * nc)
    tiles = []
    for chips in zip(*PLANE, strict=True):
        starts = [(chip // ny * nz * ny + chip % ny) * nc * own for chip in chips]
        start = jnp.where(part == 0, starts[0], starts[1]) + part * own
        for r in range(own):
            rows = pl.ds(start + r, nz, stride=ny * nc * own)
            tiles.append(jnp.concatenate([k_ref[h, 0, rows, :], k_ref[h, 1, rows, :]], axis=1))
    return halves(jnp.concatenate(tiles, axis=0))


def whole(k_ref, h):
    return halves(jnp.concatenate([k_ref[h, 0], k_ref[h, 1]], axis=1))


def tip_term(k_ref, p_ref, h, part):
    a = mul(picked_rows(k_ref, h, part), halves(p_ref[h]), NN)
    return mul(halves(a), whole(k_ref, h), NT)


def tip_kernel(inv_ref, arrow_ref, other_ref, k_ref, p_ref, sems):
    pairs = []
    for h in range(2):
        frame = arrow_ref.at[2 * h + 1]
        pairs += [(frame.at[:, pl.ds(lane * 128, 128)], k_ref.at[h, lane]) for lane in range(2)]
        pairs.append((inv_ref.at[h], p_ref.at[h]))
    copies = start_all(pairs, sems)
    part = 1 - lax.axis_index("c")
    for copy in copies[:3]:
        copy.wait()
    total = tip_term(k_ref, p_ref, 0, part)
    for copy in copies[3:]:
        copy.wait()
    other_ref[...] = total + tip_term(k_ref, p_ref, 1, part)


def tip_parts(inv_odd, arrow_blocks):
    half, order, _ = inv_odd.shape
    width = arrow_blocks.shape[1]
    return pl.pallas_call(
        tip_kernel,
        name="tip",
        out_shape=(
            jax.ShapeDtypeStruct((width // 2, width), F32),
            jax.ShapeDtypeStruct((half, 2, width, order // 2), F32),
            jax.ShapeDtypeStruct((half, order, order), F32),
        ),
        in_specs=[HBM, HBM],
        scratch_shapes=[pltpu.SemaphoreType.DMA((6,))],
        cost_estimate=pl.CostEstimate(flops=600_000_000, bytes_accessed=1_600_000, transcendentals=0),
        compiler_params=pltpu.CompilerParams(vmem_limit_bytes=24 << 20),
    )(inv_odd, arrow_blocks)


def mine_kernel(k_ref, p_ref, link_in, out_ref, link_ref, sem):
    copy = send(link_in, link_ref, sem)
    part = lax.axis_index("c")
    out_ref[...] = tip_term(k_ref, p_ref, 0, part) + tip_term(k_ref, p_ref, 1, part)
    copy.wait()


def mine_part(k, p, coupling):
    width = k.shape[2]
    return pl.pallas_call(
        mine_kernel,
        name="mine",
        out_shape=(
            jax.ShapeDtypeStruct((width // 2, width), F32),
            jax.ShapeDtypeStruct(coupling.shape, F32),
        ),
        in_specs=[VMEM, VMEM, HBM],
        out_specs=[VMEM] * 2,
        scratch_shapes=[pltpu.SemaphoreType.DMA(())],
        cost_estimate=pl.CostEstimate(flops=600_000_000, bytes_accessed=1_100_000, transcendentals=0),
        compiler_params=pltpu.CompilerParams(vmem_limit_bytes=24 << 20),
    )(k, p, coupling)


def right_kernel(k_ref, p_ref, link_ref, sent_ref):
    order = p_ref.shape[1]
    half, quarter = order // 2, order // 4
    v = halves(link_ref[3])
    w = halves(mul(halves(p_ref[1]), v, NN))
    right, low = slice(half, order), tuple(x[:, half:] for x in v)
    sent_ref[:half] = mul(tuple(x[:, :half] for x in v), w, TN)
    corner = mul(low, tuple(x[:, half:] for x in w), TN)
    sent_ref[half : half + quarter, :half] = corner[:quarter]
    sent_ref[half : half + quarter, right] = corner[quarter:]
    sent_ref[half + quarter :] = mul(whole(k_ref, 1), w, NN)


def right_parts(k, p, link):
    width, order = k.shape[2], p.shape[1]
    return pl.pallas_call(
        right_kernel,
        name="right",
        out_shape=jax.ShapeDtypeStruct((order * 3 // 4 + width, order), F32),
        in_specs=[VMEM] * 3,
        out_specs=VMEM,
        cost_estimate=pl.CostEstimate(flops=400_000_000, bytes_accessed=100_000, transcendentals=0),
        compiler_params=pltpu.CompilerParams(vmem_limit_bytes=24 << 20),
    )(k, p, link)


def add_kernel(a_ref, b_ref, out_ref, buf, sems):
    pieces = sems.shape[0]
    rows = a_ref.shape[0] // pieces
    copies = []
    for i in range(pieces):
        part = slice(i * rows, (i + 1) * rows)
        major = pl.ds(i * buf.shape[0] // pieces, buf.shape[0] // pieces)
        buf[major] = (a_ref[part] + b_ref[part]).reshape(buf.shape[0] // pieces, *buf.shape[1:])
        copies.append(pltpu.make_async_copy(buf.at[major], out_ref.at[major], sems.at[i]))
        copies[-1].start()
    for copy in copies:
        copy.wait()


def added(a, b, shape):
    return pl.pallas_call(
        add_kernel,
        name="added",
        out_shape=jax.ShapeDtypeStruct(shape, F32),
        out_specs=HBM,
        scratch_shapes=[pltpu.VMEM(shape, F32), pltpu.SemaphoreType.DMA((4,))],
        cost_estimate=pl.CostEstimate(flops=200_000, bytes_accessed=100_000, transcendentals=0),
        compiler_params=pltpu.CompilerParams(vmem_limit_bytes=16 << 20),
    )(a, b)


def fold_kernel(in_ref, out_ref):
    nz, deep, lanes = out_ref.shape
    own = in_ref.shape[1] // nz
    total = in_ref[0]
    for peer in range(1, in_ref.shape[0]):
        total = total + in_ref[peer]
    for block in range(deep // own):
        for r in range(own):
            for k, z in enumerate(COLUMN):
                row = slice(r * nz + z, r * nz + z + 1)
                out_ref[k, block * own + r : block * own + r + 1, :] = total[row, block * lanes : (block + 1) * lanes]


def folded(part, own, nz):
    deep = own * part.shape[2] // 128
    return pl.pallas_call(
        fold_kernel,
        name="folded",
        out_shape=jax.ShapeDtypeStruct((nz, deep, 128), F32),
        cost_estimate=pl.CostEstimate(flops=200_000, bytes_accessed=100_000, transcendentals=0),
        compiler_params=pltpu.CompilerParams(vmem_limit_bytes=16 << 20),
    )(part)


def final_kernel(in_ref, tip_ref, out_ref):
    total = in_ref[0]
    for peer in range(1, in_ref.shape[0]):
        total = total + in_ref[peer]
    own, cols = out_ref.shape
    for block in range(cols // 128):
        lanes = slice(block * 128, (block + 1) * 128)
        out_ref[:, lanes] = tip_ref[:, lanes] - total[block * own : (block + 1) * own]


def final(part, arrow_tip):
    return pl.pallas_call(
        final_kernel,
        name="final",
        out_shape=jax.ShapeDtypeStruct(arrow_tip.shape, F32),
        cost_estimate=pl.CostEstimate(flops=10_000, bytes_accessed=40_000, transcendentals=0),
        compiler_params=pltpu.CompilerParams(vmem_limit_bytes=16 << 20),
    )(part, arrow_tip)


def square_kernel(
    even_in, p_ref, link_ref, arrow_in, diag_ref, couple_ref, held_ref, left_ref, w_ref, arrow_ref,
    even_ref, d_out, c_out, in_sems, out_sems,
):
    copies = start_all([(even_in, even_ref)] + [(arrow_in.at[2 * h], arrow_ref.at[h]) for h in range(2)], in_sems)
    outs = []
    left, u, v = [], [], []
    for h in range(2):
        p = halves(p_ref[h])
        u.append(halves(link_ref[2 * h]))
        v.append(halves(link_ref[2 * h + 1]))
        left.append(halves(mul(u[h], p, NN)))
        left_ref[h, 0], left_ref[h, 1] = left[h]
        c_out[h] = -mul(left[h], v[h], NN)
        outs.append(send(c_out.at[h], couple_ref.at[h], out_sems.at[h]))
        if h == 0:
            w = halves(mul(p, v[0], NN))
            w_ref[0], w_ref[1] = w
    copies[0].wait()
    d_out[...] = even_ref[1] - mul(left[1], u[1], NT) - mul(v[0], w, TN)
    outs.append(send(d_out, diag_ref.at[1], out_sems.at[2]))
    held_ref[...] = even_ref[0] - mul(left[0], u[0], NT)
    for copy in copies[1:] + outs:
        copy.wait()


def square_parts(even, p, link, arrow_blocks):
    half, order, _ = p.shape
    width = arrow_blocks.shape[1]
    blocks = jax.ShapeDtypeStruct((half, order, order), F32)
    return pl.pallas_call(
        square_kernel,
        name="square",
        out_shape=(
            blocks,
            blocks,
            jax.ShapeDtypeStruct((order, order), F32),
            jax.ShapeDtypeStruct((half, 2, order, order), jnp.bfloat16),
            jax.ShapeDtypeStruct((2, order, order), jnp.bfloat16),
            jax.ShapeDtypeStruct((half, width, order), F32),
        ),
        in_specs=[HBM, VMEM, VMEM, HBM],
        out_specs=[HBM, HBM] + [VMEM] * 4,
        scratch_shapes=[
            pltpu.VMEM((half, order, order), F32),
            pltpu.VMEM((order, order), F32),
            pltpu.VMEM((half, order, order), F32),
            pltpu.SemaphoreType.DMA((3,)),
            pltpu.SemaphoreType.DMA((3,)),
        ],
        cost_estimate=pl.CostEstimate(flops=800_000_000, bytes_accessed=1_700_000, transcendentals=0),
        compiler_params=pltpu.CompilerParams(vmem_limit_bytes=24 << 20),
    )(even, p, link, arrow_blocks)


def tall_kernel(arrow_ref, k_ref, left_ref, w_ref, new_ref, held_ref, a_out, sem):
    later = mul(whole(k_ref, 1), (left_ref[1, 0], left_ref[1, 1]), NT)
    k = whole(k_ref, 0)
    a_out[...] = arrow_ref[1] - (later + mul(k, (w_ref[0], w_ref[1]), NN))
    out = send(a_out, new_ref.at[1], sem)
    held_ref[...] = arrow_ref[0] - mul(k, (left_ref[0, 0], left_ref[0, 1]), NT)
    out.wait()


def tall_parts(arrow_even, k, left, w):
    half, width, order = arrow_even.shape
    return pl.pallas_call(
        tall_kernel,
        name="tall",
        out_shape=(
            jax.ShapeDtypeStruct((half, width, order), F32),
            jax.ShapeDtypeStruct((width, order), F32),
        ),
        in_specs=[VMEM] * 4,
        out_specs=[HBM, VMEM],
        scratch_shapes=[pltpu.VMEM((width, order), F32), pltpu.SemaphoreType.DMA(())],
        cost_estimate=pl.CostEstimate(flops=600_000_000, bytes_accessed=600_000, transcendentals=0),
        compiler_params=pltpu.CompilerParams(vmem_limit_bytes=24 << 20),
    )(arrow_even, k, left, w)


def settle_kernel(diag_ref, new_ref, square_ref, tall_ref, got_in, diag_out, new_out, d_buf, a_buf, g_buf, in_sems, sems):
    del diag_ref, new_ref
    order = got_in.shape[1]
    half, quarter = order // 2, order // 4
    head, width = half + quarter, a_buf.shape[0]
    rows = width // 2
    cuts = [pl.ds(0, head), pl.ds(head, rows), pl.ds(head + rows, rows)]
    copies = start_all([(got_in.at[cut], g_buf.at[cut]) for cut in cuts], in_sems)
    outs = []
    copies[0].wait()
    top = g_buf[:half]
    d_buf[:half] = square_ref[:half] - top
    d_buf[half:, :half] = square_ref[half:, :half] - top[:, half:].T
    d_buf[half:head, half:] = square_ref[half:head, half:] - g_buf[half:head, :half]
    d_buf[head:, half:] = square_ref[head:, half:] - g_buf[half:head, half:]
    outs.append(send(d_buf, diag_out.at[0], sems.at[0]))
    for i in range(2):
        copies[1 + i].wait()
        here = slice(i * rows, (i + 1) * rows)
        a_buf[here] = tall_ref[here] - g_buf[head + i * rows : head + (i + 1) * rows]
        part = pl.ds(i * rows, rows)
        outs.append(send(a_buf.at[part], new_out.at[0, part], sems.at[1 + i]))
    for copy in outs:
        copy.wait()


def settle(diag_part, arrow_part, square, tall, received):
    return pl.pallas_call(
        settle_kernel,
        name="settle",
        out_shape=(
            jax.ShapeDtypeStruct(diag_part.shape, F32),
            jax.ShapeDtypeStruct(arrow_part.shape, F32),
        ),
        in_specs=[HBM, HBM, VMEM, VMEM, HBM],
        out_specs=[HBM] * 2,
        input_output_aliases={0: 0, 1: 1},
        scratch_shapes=[
            pltpu.VMEM(square.shape, F32),
            pltpu.VMEM(tall.shape, F32),
            pltpu.VMEM(received.shape, F32),
            pltpu.SemaphoreType.DMA((3,)),
            pltpu.SemaphoreType.DMA((3,)),
        ],
        cost_estimate=pl.CostEstimate(flops=200_000, bytes_accessed=1_500_000, transcendentals=0),
        compiler_params=pltpu.CompilerParams(vmem_limit_bytes=16 << 20),
    )(diag_part, arrow_part, square, tall, received)


def place(x, z, y, core):
    _, nz, ny, nc = SIZES
    return ((x * nz + z) * ny + y) * nc + core


def plane_groups():
    _, nz, ny, nc = SIZES
    return [[place(chip // ny, z, chip % ny, core) for chip in PLANE[core]] for z in range(nz) for core in range(nc)]


def column_groups():
    nx, _, ny, nc = SIZES
    return [[place(x, z, y, core) for z in COLUMN] for x in range(nx) for y in range(ny) for core in range(nc)]


def shifted(x, by):
    count = 1
    for size in SIZES:
        count *= size
    pairs = [(i, i + by) for i in range(count) if 0 <= i + by < count]
    return lax.ppermute(x, AXES, pairs)


def per_device(diag_even, inv_odd, coupling, arrow_blocks, arrow_tip):
    own, cols = arrow_tip.shape
    nx, nz, ny, _ = SIZES
    diag_even, inv_odd, coupling, arrow_blocks = (
        pltpu.with_memory_space_constraint(x, pltpu.HBM) for x in (diag_even, inv_odd, coupling, arrow_blocks)
    )
    other, k_kept, p_kept = tip_parts(inv_odd, arrow_blocks)
    got = lax.ppermute(other, "c", [(0, 1), (1, 0)])
    mine, link = mine_part(k_kept, p_kept, coupling)
    part = added(mine, got, (nx * ny, own * nz, cols))
    part = lax.all_to_all(part, AXES, 0, 0, axis_index_groups=plane_groups(), tiled=True)
    sent = right_parts(k_kept, p_kept, link)
    diag_part, couple_new, square, left, w, arrow_even = square_parts(diag_even, p_kept, link, arrow_blocks)
    received = shifted(sent, 1)
    arrow_part, tall = tall_parts(arrow_even, k_kept, left, w)
    part = folded(part, own, nz)
    part = lax.all_to_all(part, AXES, 0, 0, axis_index_groups=column_groups(), tiled=True)
    tip_new = final(part, arrow_tip)
    diag_new, arrow_new = settle(diag_part, arrow_part, square, tall, received)
    return (diag_new, couple_new, arrow_new, tip_new)


def solution(mesh):
    torus = Mesh(mesh.devices.reshape(SIZES), AXES)
    cube = P(AXES, None, None)
    flat = P(AXES, None)

    return jax.shard_map(
        per_device,
        mesh=torus,
        in_specs=(cube, cube, cube, cube, flat),
        out_specs=(cube, cube, cube, flat),
        check_vma=False,
    )
```

```python
import functools

import jax
import jax.numpy as jnp
from jax import lax
from jax.experimental import pallas as pl
from jax.experimental.pallas import tpu as pltpu
from jax.sharding import Mesh
from jax.sharding import PartitionSpec as P

AXES = ("x", "z", "y", "c")
SIZES = (4, 8, 4, 2)
PLANE = (
    (14, 1, 3, 15, 8, 0, 7, 9, 6, 4, 13, 5, 11, 2, 12, 10),
    (10, 6, 4, 9, 15, 12, 2, 11, 14, 7, 1, 13, 8, 0, 5, 3),
)
COLUMN = (4, 0, 1, 7, 2, 6, 3, 5)
F32 = jnp.float32
NN = (((1,), (0,)), ((), ()))
NT = (((1,), (1,)), ((), ()))
TN = (((0,), (0,)), ((), ()))
HBM = pl.BlockSpec(memory_space=pltpu.HBM)
VMEM = pl.BlockSpec(memory_space=pltpu.VMEM)


def halves(x):
    high = x.astype(jnp.bfloat16)
    return high, (x - high.astype(F32)).astype(jnp.bfloat16)


def mul(a, b, dims):
    dot = functools.partial(lax.dot_general, dimension_numbers=dims, preferred_element_type=F32)
    return dot(a[0], b[0]) + (dot(a[0], b[1]) + dot(a[1], b[0]))


def start_all(pairs, sems):
    copies = [pltpu.make_async_copy(src, dst, sems.at[i]) for i, (src, dst) in enumerate(pairs)]
    for copy in copies:
        copy.start()
    return copies


def send(src, dst, sem):
    copy = pltpu.make_async_copy(src, dst, sem)
    copy.start()
    return copy


def picked_rows(k_ref, h, part):
    nx, nz, ny, nc = SIZES
    own = k_ref.shape[2] // (nx * nz * ny * nc)
    tiles = []
    for chips in zip(*PLANE, strict=True):
        starts = [(chip // ny * nz * ny + chip % ny) * nc * own for chip in chips]
        start = jnp.where(part == 0, starts[0], starts[1]) + part * own
        for r in range(own):
            rows = pl.ds(start + r, nz, stride=ny * nc * own)
            tiles.append(jnp.concatenate([k_ref[h, 0, rows, :], k_ref[h, 1, rows, :]], axis=1))
    return halves(jnp.concatenate(tiles, axis=0))


def whole(k_ref, h):
    return halves(jnp.concatenate([k_ref[h, 0], k_ref[h, 1]], axis=1))


def tip_term(k_ref, p_ref, h, part):
    a = mul(picked_rows(k_ref, h, part), halves(p_ref[h]), NN)
    return mul(halves(a), whole(k_ref, h), NT)


def tip_kernel(inv_ref, arrow_ref, other_ref, k_ref, p_ref, sems):
    pairs = []
    for h in range(2):
        frame = arrow_ref.at[2 * h + 1]
        pairs += [(frame.at[:, pl.ds(lane * 128, 128)], k_ref.at[h, lane]) for lane in range(2)]
        pairs.append((inv_ref.at[h], p_ref.at[h]))
    copies = start_all(pairs, sems)
    part = 1 - lax.axis_index("c")
    for copy in copies[:3]:
        copy.wait()
    total = tip_term(k_ref, p_ref, 0, part)
    for copy in copies[3:]:
        copy.wait()
    other_ref[...] = total + tip_term(k_ref, p_ref, 1, part)


def tip_parts(inv_odd, arrow_blocks):
    half, order, _ = inv_odd.shape
    width = arrow_blocks.shape[1]
    return pl.pallas_call(
        tip_kernel,
        name="tip",
        out_shape=(
            jax.ShapeDtypeStruct((width // 2, width), F32),
            jax.ShapeDtypeStruct((half, 2, width, order // 2), F32),
            jax.ShapeDtypeStruct((half, order, order), F32),
        ),
        in_specs=[HBM, HBM],
        scratch_shapes=[pltpu.SemaphoreType.DMA((6,))],
        cost_estimate=pl.CostEstimate(flops=600_000_000, bytes_accessed=1_600_000, transcendentals=0),
        compiler_params=pltpu.CompilerParams(vmem_limit_bytes=24 << 20),
    )(inv_odd, arrow_blocks)


def mine_kernel(k_ref, p_ref, link_in, out_ref, link_ref, sem):
    copy = send(link_in, link_ref, sem)
    part = lax.axis_index("c")
    out_ref[...] = tip_term(k_ref, p_ref, 0, part) + tip_term(k_ref, p_ref, 1, part)
    copy.wait()


def mine_part(k, p, coupling):
    width = k.shape[2]
    return pl.pallas_call(
        mine_kernel,
        name="mine",
        out_shape=(
            jax.ShapeDtypeStruct((width // 2, width), F32),
            jax.ShapeDtypeStruct(coupling.shape, F32),
        ),
        in_specs=[VMEM, VMEM, HBM],
        out_specs=[VMEM] * 2,
        scratch_shapes=[pltpu.SemaphoreType.DMA(())],
        cost_estimate=pl.CostEstimate(flops=600_000_000, bytes_accessed=1_100_000, transcendentals=0),
        compiler_params=pltpu.CompilerParams(vmem_limit_bytes=24 << 20),
    )(k, p, coupling)


def right_kernel(k_ref, p_ref, link_ref, sent_ref):
    order = p_ref.shape[1]
    half, quarter = order // 2, order // 4
    v = halves(link_ref[3])
    w = halves(mul(halves(p_ref[1]), v, NN))
    right, low = slice(half, order), tuple(x[:, half:] for x in v)
    sent_ref[:half] = mul(tuple(x[:, :half] for x in v), w, TN)
    corner = mul(low, tuple(x[:, half:] for x in w), TN)
    sent_ref[half : half + quarter, :half] = corner[:quarter]
    sent_ref[half : half + quarter, right] = corner[quarter:]
    sent_ref[half + quarter :] = mul(whole(k_ref, 1), w, NN)


def right_parts(k, p, link):
    width, order = k.shape[2], p.shape[1]
    return pl.pallas_call(
        right_kernel,
        name="right",
        out_shape=jax.ShapeDtypeStruct((order * 3 // 4 + width, order), F32),
        in_specs=[VMEM] * 3,
        out_specs=VMEM,
        cost_estimate=pl.CostEstimate(flops=400_000_000, bytes_accessed=100_000, transcendentals=0),
        compiler_params=pltpu.CompilerParams(vmem_limit_bytes=24 << 20),
    )(k, p, link)


def add_kernel(a_ref, b_ref, out_ref, buf, sems):
    pieces = sems.shape[0]
    rows = a_ref.shape[0] // pieces
    copies = []
    for i in range(pieces):
        part = slice(i * rows, (i + 1) * rows)
        major = pl.ds(i * buf.shape[0] // pieces, buf.shape[0] // pieces)
        buf[major] = (a_ref[part] + b_ref[part]).reshape(buf.shape[0] // pieces, *buf.shape[1:])
        copies.append(pltpu.make_async_copy(buf.at[major], out_ref.at[major], sems.at[i]))
        copies[-1].start()
    for copy in copies:
        copy.wait()


def added(a, b, shape):
    return pl.pallas_call(
        add_kernel,
        name="added",
        out_shape=jax.ShapeDtypeStruct(shape, F32),
        out_specs=HBM,
        scratch_shapes=[pltpu.VMEM(shape, F32), pltpu.SemaphoreType.DMA((4,))],
        cost_estimate=pl.CostEstimate(flops=200_000, bytes_accessed=100_000, transcendentals=0),
        compiler_params=pltpu.CompilerParams(vmem_limit_bytes=16 << 20),
    )(a, b)


def fold_kernel(in_ref, out_ref):
    nz, deep, lanes = out_ref.shape
    own = in_ref.shape[1] // nz
    total = in_ref[0]
    for peer in range(1, in_ref.shape[0]):
        total = total + in_ref[peer]
    for block in range(deep // own):
        for r in range(own):
            for k, z in enumerate(COLUMN):
                row = slice(r * nz + z, r * nz + z + 1)
                out_ref[k, block * own + r : block * own + r + 1, :] = total[row, block * lanes : (block + 1) * lanes]


def folded(part, own, nz):
    deep = own * part.shape[2] // 128
    return pl.pallas_call(
        fold_kernel,
        name="folded",
        out_shape=jax.ShapeDtypeStruct((nz, deep, 128), F32),
        cost_estimate=pl.CostEstimate(flops=200_000, bytes_accessed=100_000, transcendentals=0),
        compiler_params=pltpu.CompilerParams(vmem_limit_bytes=16 << 20),
    )(part)


def final_kernel(in_ref, tip_ref, out_ref):
    total = in_ref[0]
    for peer in range(1, in_ref.shape[0]):
        total = total + in_ref[peer]
    own, cols = out_ref.shape
    for block in range(cols // 128):
        lanes = slice(block * 128, (block + 1) * 128)
        out_ref[:, lanes] = tip_ref[:, lanes] - total[block * own : (block + 1) * own]


def final(part, arrow_tip):
    return pl.pallas_call(
        final_kernel,
        name="final",
        out_shape=jax.ShapeDtypeStruct(arrow_tip.shape, F32),
        cost_estimate=pl.CostEstimate(flops=10_000, bytes_accessed=40_000, transcendentals=0),
        compiler_params=pltpu.CompilerParams(vmem_limit_bytes=16 << 20),
    )(part, arrow_tip)


def square_kernel(
    even_in, p_ref, link_ref, arrow_in, diag_ref, couple_ref, held_ref, left_ref, w_ref, arrow_ref,
    even_ref, d_out, c_out, in_sems, out_sems,
):
    copies = start_all([(even_in, even_ref)] + [(arrow_in.at[2 * h], arrow_ref.at[h]) for h in range(2)], in_sems)
    outs = []
    left, u, v = [], [], []
    for h in range(2):
        p = halves(p_ref[h])
        u.append(halves(link_ref[2 * h]))
        v.append(halves(link_ref[2 * h + 1]))
        left.append(halves(mul(u[h], p, NN)))
        left_ref[h, 0], left_ref[h, 1] = left[h]
        c_out[h] = -mul(left[h], v[h], NN)
        outs.append(send(c_out.at[h], couple_ref.at[h], out_sems.at[h]))
        if h == 0:
            w = halves(mul(p, v[0], NN))
            w_ref[0], w_ref[1] = w
    copies[0].wait()
    d_out[...] = even_ref[1] - mul(left[1], u[1], NT) - mul(v[0], w, TN)
    outs.append(send(d_out, diag_ref.at[1], out_sems.at[2]))
    held_ref[...] = even_ref[0] - mul(left[0], u[0], NT)
    for copy in copies[1:] + outs:
        copy.wait()


def square_parts(even, p, link, arrow_blocks):
    half, order, _ = p.shape
    width = arrow_blocks.shape[1]
    blocks = jax.ShapeDtypeStruct((half, order, order), F32)
    return pl.pallas_call(
        square_kernel,
        name="square",
        out_shape=(
            blocks,
            blocks,
            jax.ShapeDtypeStruct((order, order), F32),
            jax.ShapeDtypeStruct((half, 2, order, order), jnp.bfloat16),
            jax.ShapeDtypeStruct((2, order, order), jnp.bfloat16),
            jax.ShapeDtypeStruct((half, width, order), F32),
        ),
        in_specs=[HBM, VMEM, VMEM, HBM],
        out_specs=[HBM, HBM] + [VMEM] * 4,
        scratch_shapes=[
            pltpu.VMEM((half, order, order), F32),
            pltpu.VMEM((order, order), F32),
            pltpu.VMEM((half, order, order), F32),
            pltpu.SemaphoreType.DMA((3,)),
            pltpu.SemaphoreType.DMA((3,)),
        ],
        cost_estimate=pl.CostEstimate(flops=800_000_000, bytes_accessed=1_700_000, transcendentals=0),
        compiler_params=pltpu.CompilerParams(vmem_limit_bytes=24 << 20),
    )(even, p, link, arrow_blocks)


def tall_kernel(arrow_ref, k_ref, left_ref, w_ref, new_ref, held_ref, a_out, sem):
    later = mul(whole(k_ref, 1), (left_ref[1, 0], left_ref[1, 1]), NT)
    k = whole(k_ref, 0)
    a_out[...] = arrow_ref[1] - (later + mul(k, (w_ref[0], w_ref[1]), NN))
    out = send(a_out, new_ref.at[1], sem)
    held_ref[...] = arrow_ref[0] - mul(k, (left_ref[0, 0], left_ref[0, 1]), NT)
    out.wait()


def tall_parts(arrow_even, k, left, w):
    half, width, order = arrow_even.shape
    return pl.pallas_call(
        tall_kernel,
        name="tall",
        out_shape=(
            jax.ShapeDtypeStruct((half, width, order), F32),
            jax.ShapeDtypeStruct((width, order), F32),
        ),
        in_specs=[VMEM] * 4,
        out_specs=[HBM, VMEM],
        scratch_shapes=[pltpu.VMEM((width, order), F32), pltpu.SemaphoreType.DMA(())],
        cost_estimate=pl.CostEstimate(flops=600_000_000, bytes_accessed=600_000, transcendentals=0),
        compiler_params=pltpu.CompilerParams(vmem_limit_bytes=24 << 20),
    )(arrow_even, k, left, w)


def settle_kernel(diag_ref, new_ref, square_ref, tall_ref, got_in, diag_out, new_out, d_buf, a_buf, g_buf, in_sems, sems):
    del diag_ref, new_ref
    order = got_in.shape[1]
    half, quarter = order // 2, order // 4
    head, width = half + quarter, a_buf.shape[0]
    rows = width // 2
    cuts = [pl.ds(0, head), pl.ds(head, rows), pl.ds(head + rows, rows)]
    copies = start_all([(got_in.at[cut], g_buf.at[cut]) for cut in cuts], in_sems)
    outs = []
    copies[0].wait()
    top = g_buf[:half]
    d_buf[:half] = square_ref[:half] - top
    d_buf[half:, :half] = square_ref[half:, :half] - top[:, half:].T
    d_buf[half:head, half:] = square_ref[half:head, half:] - g_buf[half:head, :half]
    d_buf[head:, half:] = square_ref[head:, half:] - g_buf[half:head, half:]
    outs.append(send(d_buf, diag_out.at[0], sems.at[0]))
    for i in range(2):
        copies[1 + i].wait()
        here = slice(i * rows, (i + 1) * rows)
        a_buf[here] = tall_ref[here] - g_buf[head + i * rows : head + (i + 1) * rows]
        part = pl.ds(i * rows, rows)
        outs.append(send(a_buf.at[part], new_out.at[0, part], sems.at[1 + i]))
    for copy in outs:
        copy.wait()


def settle(diag_part, arrow_part, square, tall, received):
    return pl.pallas_call(
        settle_kernel,
        name="settle",
        out_shape=(
            jax.ShapeDtypeStruct(diag_part.shape, F32),
            jax.ShapeDtypeStruct(arrow_part.shape, F32),
        ),
        in_specs=[HBM, HBM, VMEM, VMEM, HBM],
        out_specs=[HBM] * 2,
        input_output_aliases={0: 0, 1: 1},
        scratch_shapes=[
            pltpu.VMEM(square.shape, F32),
            pltpu.VMEM(tall.shape, F32),
            pltpu.VMEM(received.shape, F32),
            pltpu.SemaphoreType.DMA((3,)),
            pltpu.SemaphoreType.DMA((3,)),
        ],
        cost_estimate=pl.CostEstimate(flops=200_000, bytes_accessed=1_500_000, transcendentals=0),
        compiler_params=pltpu.CompilerParams(vmem_limit_bytes=16 << 20),
    )(diag_part, arrow_part, square, tall, received)


def place(x, z, y, core):
    _, nz, ny, nc = SIZES
    return ((x * nz + z) * ny + y) * nc + core


def plane_groups():
    _, nz, ny, nc = SIZES
    return [[place(chip // ny, z, chip % ny, core) for chip in PLANE[core]] for z in range(nz) for core in range(nc)]


def column_groups():
    nx, _, ny, nc = SIZES
    return [[place(x, z, y, core) for z in COLUMN] for x in range(nx) for y in range(ny) for core in range(nc)]


def shifted(x, by):
    count = 1
    for size in SIZES:
        count *= size
    pairs = [(i, i + by) for i in range(count) if 0 <= i + by < count]
    return lax.ppermute(x, AXES, pairs)


def per_device(diag_even, inv_odd, coupling, arrow_blocks, arrow_tip):
    own, cols = arrow_tip.shape
    nx, nz, ny, _ = SIZES
    diag_even, inv_odd, coupling, arrow_blocks = (
        pltpu.with_memory_space_constraint(x, pltpu.HBM) for x in (diag_even, inv_odd, coupling, arrow_blocks)
    )
    other, k_kept, p_kept = tip_parts(inv_odd, arrow_blocks)
    got = lax.ppermute(other, "c", [(0, 1), (1, 0)])
    mine, link = mine_part(k_kept, p_kept, coupling)
    part = added(mine, got, (nx * ny, own * nz, cols))
    part = lax.all_to_all(part, AXES, 0, 0, axis_index_groups=plane_groups(), tiled=True)
    sent = right_parts(k_kept, p_kept, link)
    diag_part, couple_new, square, left, w, arrow_even = square_parts(diag_even, p_kept, link, arrow_blocks)
    received = shifted(sent, 1)
    arrow_part, tall = tall_parts(arrow_even, k_kept, left, w)
    part = folded(part, own, nz)
    part = lax.all_to_all(part, AXES, 0, 0, axis_index_groups=column_groups(), tiled=True)
    tip_new = final(part, arrow_tip)
    diag_new, arrow_new = settle(diag_part, arrow_part, square, tall, received)
    return (diag_new, couple_new, arrow_new, tip_new)


def solution(mesh):
    torus = Mesh(mesh.devices.reshape(SIZES), AXES)
    cube = P(AXES, None, None)
    flat = P(AXES, None)

    return jax.shard_map(
        per_device,
        mesh=torus,
        in_specs=(cube, cube, cube, cube, flat),
        out_specs=(cube, cube, cube, flat),
        check_vma=False,
    )
```
